256 devices in a mesh: lat: 4 (over y), lon: 64 (over z, x, core).
Axes of the slice: x: 4, y: 4, z: 8, core: 2. Of those that a mesh axis runs over, the one named last changes fastest.
Arguments:
- field: float32 [64, 16384, 128], P('lat', 'lon'), may hold values from -6 to 6
- ocean: int32 [64, 16384], P('lat', 'lon'), may hold values 0 or 1
- modes: int32 [128], replicated, may hold values from 1 to 8191, as said below
- spectral_weight: float32 [128, 2, 128, 128], P('lon'), may hold values from -0.375 to 0.375
- local_weight: float32 [128, 128], replicated, may hold values from -0.5 to 0.5
- layer_bias: float32 [128], replicated, may hold values from -4 to 4
- conv_weight: float32 [3, 3, 128, 128], replicated, may hold values from -0.1875 to 0.1875
- conv_bias: float32 [128], replicated, may hold values from -2 to 2
Outputs:
- decoded: float32 [64, 16384, 128], P('lat', 'lon')
The draws below stay inside these ranges and needn't reach their ends.
Inputs may be any that keep to these rules, and one draw needn't show every extreme that they name: `modes`: distinct wavenumbers.
All inputs are finite; a program needn't handle non-finite values. No bound on the sum of `ocean` on one device may be relied on, other than what follows from the above.
Results may differ from the reference program's by a relative error of at most 0.0001.
Values sent between devices are 32-bit elements; how exact they have to be, the bound alone decides.
A program may use at most 64 MiB of HBM per device.

```python
import math
import jax
import jax.numpy as jnp
from jax import lax

C = 128
NLAT = 64
NLON = 16384
MODES = 128


def draw_modes(key, part):
    return (jax.random.permutation(key, NLON // 2 - 1)[:MODES] + 1).astype(jnp.int32)


def with_ends(array, key, least, top_value):
    extent = array.shape
    spot = [jax.random.randint(jax.random.fold_in(key, axis), (), 0, extent[axis]) for axis in range(len(extent))]
    array = array.at[tuple(spot)].set(least)
    longest = extent.index(max(extent))
    spot[longest] = (spot[longest] + 1) % extent[longest]
    return array.at[tuple(spot)].set(top_value)


def level_of(key, extent, cuts, low, largest):
    def one(position, blocks):
        draws = jax.random.uniform(jax.random.fold_in(jax.random.fold_in(key, 6), position), (blocks,), jnp.float32, low / len(cuts), largest / len(cuts))
        return jnp.repeat(jnp.exp(draws), extent[position] // blocks).reshape((-1,) + (1,) * (len(extent) - position - 1))

    level = one(*cuts[0])
    for cut in cuts[1:]:
        level = level * one(*cut)
    return level


def noise(rng, extent, spread, limit, cuts=(), kind=jnp.bfloat16):
    loudness = level_of(rng, extent, cuts, -0.22, 0.18) if cuts else 1.0
    result = jax.random.normal(rng, extent, jnp.float32) * spread * loudness
    return jnp.minimum(jnp.maximum(result, -limit), limit).astype(kind)


def setup_inputs(seed: int = 0) -> dict:
    arg_keys = jax.random.split(jax.random.key(seed), 9)
    field = noise(arg_keys[0], (NLAT, NLON, C), 1.0, 6.0, ((0, 4), (1, 64)), jnp.float32)
    ocean = with_ends((jax.random.randint(arg_keys[1], (NLAT, NLON), 0, 3) < 2).astype(jnp.int32), jax.random.fold_in(arg_keys[1], 1), 0, 1)
    modes = draw_modes(jax.random.fold_in(arg_keys[8], 71), 0)
    spectral_weight = noise(arg_keys[3], (MODES, 2, C, C), (2 * C) ** -0.5, 0.375, ((0, 64),), jnp.float32)
    local_weight = noise(arg_keys[4], (C, C), C ** -0.5, 0.5, (), jnp.float32)
    layer_bias = noise(arg_keys[5], (C,), 1.0, 4.0, (), jnp.float32)
    conv_weight = noise(arg_keys[6], (3, 3, C, C), (9 * C) ** -0.5, 0.1875, (), jnp.float32)
    conv_bias = noise(arg_keys[7], (C,), 0.5, 2.0, (), jnp.float32)
    return dict(field=field, ocean=ocean, modes=modes, spectral_weight=spectral_weight, local_weight=local_weight, layer_bias=layer_bias, conv_weight=conv_weight, conv_bias=conv_bias)


HIGH = lax.Precision.HIGHEST

def reference(field, ocean, modes, spectral_weight, local_weight, layer_bias, conv_weight, conv_bias):
    lon_ids = jnp.arange(NLON, dtype=jnp.int32)
    product = modes[:, None] * lon_ids[None, :] % NLON
    theta = product.astype(jnp.float32) * (2.0 * math.pi / NLON)
    cosine = jnp.cos(theta)
    sine = jnp.sin(theta)
    real_part = jnp.einsum('mj,ijc->mic', cosine, field, precision=HIGH) / math.sqrt(NLON)
    imag_part = -jnp.einsum('mj,ijc->mic', sine, field, precision=HIGH) / math.sqrt(NLON)
    coeffs = jnp.concatenate([real_part, imag_part], -1)
    w_real = spectral_weight[:, 0]
    w_imag = spectral_weight[:, 1]
    upper = jnp.concatenate([w_real, w_imag], -1)
    lower = jnp.concatenate([-w_imag, w_real], -1)
    blocks = jnp.concatenate([upper, lower], 1)
    mixed = jnp.einsum('mic,mcd->mid', coeffs, blocks, precision=HIGH)
    spectral = jnp.einsum('mj,mic->ijc', cosine, mixed[:, :, :C], precision=HIGH)
    spectral = spectral - jnp.einsum('mj,mic->ijc', sine, mixed[:, :, C:], precision=HIGH)
    spectral = spectral * (2.0 / math.sqrt(MODES))
    wet = ocean.astype(jnp.float32)[:, :, None]
    local = jnp.einsum('ijc,cd->ijd', field, local_weight, precision=HIGH)
    hidden = wet * jax.nn.gelu(spectral + local + layer_bias, approximate=True)
    padded = jnp.concatenate([hidden[:, -1:], hidden, hidden[:, :1]], 1)
    padded = jnp.pad(padded, ((1, 1), (0, 0), (0, 0)))

    def one_row(index):
        block = lax.dynamic_slice_in_dim(padded, index, 3, 0)
        total = jnp.zeros((NLON, C), jnp.float32)
        for row_tap in range(3):
            for col_tap in range(3):
                total = total + jnp.dot(block[row_tap, col_tap:col_tap + NLON], conv_weight[row_tap, col_tap], precision=HIGH)
        return total
    conv = lax.map(one_row, jnp.arange(NLAT, dtype=jnp.int32))
    return wet * (conv + conv_bias)
```

```python
import functools
import math

import jax
import jax.numpy as jnp
from jax import lax
from jax.experimental import pallas as pl
from jax.experimental.pallas import tpu as pltpu
from jax.sharding import Mesh
from jax.sharding import PartitionSpec as P

LON = ("lon_0", "lon_1", "lon_2")
HIGH = lax.Precision.HIGHEST
PAD = 8
BF = jnp.bfloat16
F32 = jnp.float32


def split_up(value, dim, size):
    dims = value.shape
    blocks = value.reshape(*dims[:dim], size, dims[dim] // size, *dims[dim + 1 :])
    return jnp.moveaxis(blocks, dim, 0)


def sent_and_summed(value, axis, dim):
    size = lax.axis_size(axis)
    blocks = lax.all_to_all(split_up(value, dim, size), axis, 0, 0, tiled=True)
    return jnp.sum(blocks, axis=0)


def sum_by_axis(value, axes, dim):
    far, near = axes
    own = sent_and_summed(split_up(value, dim, lax.axis_size(far)), near, dim + 1)
    return jnp.sum(lax.all_to_all(own, far, 0, 0, tiled=True), axis=0)


def sent_to_all(value, axis):
    copies = jnp.broadcast_to(value, (lax.axis_size(axis), *value.shape))
    return lax.all_to_all(copies, axis, split_axis=0, concat_axis=0, tiled=True)


def joined_along(blocks, dim):
    blocks = jnp.moveaxis(blocks, 0, dim)
    dims = blocks.shape
    return blocks.reshape(*dims[:dim], dims[dim] * dims[dim + 1], *dims[dim + 2 :])


def whole_of(value, axes, dim):
    far, near = axes
    blocks = sent_to_all(sent_to_all(value, far), near)
    return joined_along(blocks.swapaxes(0, 1).reshape(-1, *value.shape), dim)


def with_halo(block, sides, width, periodic):
    for axis, dim in sides:
        count = lax.axis_size(axis)
        forward = [(i, i + 1) for i in range(count - 1)]
        if periodic:
            forward.append((count - 1, 0))
        backward = [(target, source) for source, target in forward]
        low = lax.ppermute(
            lax.slice_in_dim(block, block.shape[dim] - width, None, axis=dim), axis, forward
        )
        high = lax.ppermute(lax.slice_in_dim(block, 0, width, axis=dim), axis, backward)
        block = jnp.concatenate([low, block, high], axis=dim)
    return block


def mix_modes(coeffs, weights):
    w_real = weights[:, 0]
    w_imag = weights[:, 1]
    upper = jnp.concatenate([w_real, w_imag], -1)
    lower = jnp.concatenate([-w_imag, w_real], -1)
    blocks = jnp.concatenate([upper, lower], 1)
    return jnp.einsum("mic,mcd->mid", coeffs, blocks, precision=HIGH)


def halves(value):
    high = value.astype(BF)
    return high, (value - high.astype(F32)).astype(BF)


def stored_halves(value):
    high = lax.reduce_precision(value, 8, 7)
    return high.astype(BF), (value - high).astype(BF)


def dot(a, b):
    return jnp.dot(a, b, preferred_element_type=F32)


def lane_sum(acc):
    return acc[:, :128] + acc[:, 128:]


def tail_kernel(
    rows, width, scale, lat_axis, lat_count,
    mixed_hbm, field_hbm, wet_ref, table_ref, local_ref, bias_ref, conv_ref, conv_bias_ref,
    out_hbm,
    mixed, field, hidden, mask, taps, local, out, sem_in, sem_out,
):
    ext = rows + 2
    wide = width + 2 * PAD
    half = rows // 2

    def mixed_copy(r):
        part, block = (1, half) if r == 0 else (0, half) if r == ext - 1 else divmod(r - 1, half)
        source = mixed_hbm.at[part, :, pl.ds(block * 128, 128)]
        return pltpu.make_async_copy(source, mixed.at[r], sem_in.at[0, r])

    def field_copy(r):
        return pltpu.make_async_copy(field_hbm.at[r], field.at[r], sem_in.at[1, r])

    for r in range(ext):
        mixed_copy(r).start()
        field_copy(r).start()

    high, low = halves(local_ref[...])
    both = jnp.concatenate([high, low], 1)
    local[0:128] = both
    local[128:256] = both
    for a in range(3):
        for b in range(3):
            high, low = halves(conv_ref[a, b])
            both = jnp.concatenate([high, low], 1)
            for q in range(2):
                taps[pl.ds(a * 256 + q * 128, 128), pl.ds(b * 256, 256)] = both

    lane = lax.broadcasted_iota(jnp.int32, (wide, 128), 1)
    lat = lax.axis_index(lat_axis)
    above = jnp.where(lat > 0, 1.0, 0.0).astype(F32)
    below = jnp.where(lat < lat_count - 1, 1.0, 0.0).astype(F32)
    top = pltpu.roll(wet_ref[0], 128 - rows, 1) * above
    bottom = pltpu.roll(wet_ref[2], rows, 1) * below
    wet = jnp.where(lane == 0, top, jnp.where(lane == rows + 1, bottom, wet_ref[1])).astype(BF)

    @pl.loop(0, ext)
    def _(r):
        pltpu.make_async_copy(field_hbm.at[0], field.at[0], sem_in.at[1, r]).wait()
        pltpu.make_async_copy(
            mixed_hbm.at[0, :, pl.ds(0, 128)], mixed.at[0], sem_in.at[0, r]
        ).wait()
        high, low = halves(mixed[r])
        both = jnp.concatenate([high, low], 1)
        spectral = lane_sum(dot(table_ref[...], jnp.concatenate([both, both], 0))) * scale
        high, low = halves(field[r])
        point = lane_sum(dot(jnp.concatenate([high, low], 1), local[...]))
        pick = lax.broadcasted_iota(jnp.int32, (128, 128), 0) == r
        cover = dot(wet, pick.astype(F32).astype(BF))
        mask[r] = cover
        value = cover * jax.nn.gelu(spectral + point + bias_ref[...], approximate=True)
        high, low = halves(value)
        both = jnp.concatenate([high, low], 1)
        for a in range(3):
            hidden[r + 2 - a, :, pl.ds(a * 256, 256)] = both

    group = 2

    @pl.loop(0, rows // group)
    def _(t):
        i = t * group
        block = hidden[pl.ds(i + 2, group)].reshape(group * wide, 768)
        left, middle, right = (
            lane_sum(dot(block, taps[:, pl.ds(b * 256, 256)])) for b in range(3)
        )
        total = pltpu.roll(left, 1, 0) + middle + pltpu.roll(right, group * wide - 1, 0)
        total = (total + conv_bias_ref[...]).reshape(group, wide, 128)
        total = total * mask[pl.ds(i + 1, group)]
        out[pl.ds(i, group)] = total[:, PAD : PAD + width]
        pltpu.make_async_copy(
            out.at[pl.ds(i, group)], out_hbm.at[pl.ds(i, group)], sem_out.at[t]
        ).start()

    @pl.loop(0, rows // group)
    def _(t):
        pltpu.make_async_copy(
            out.at[pl.ds(0, group)], out_hbm.at[pl.ds(0, group)], sem_out.at[t]
        ).wait()


def tail(mixed, field, wet, table, local_weight, layer_bias, conv_weight, conv_bias, rows, width, scale, lat_axis, lat_count):
    ext = rows + 2
    wide = width + 2 * PAD
    vmem = pl.BlockSpec(memory_space=pltpu.VMEM)
    hbm = pl.BlockSpec(memory_space=pl.ANY)
    return pl.pallas_call(
        functools.partial(tail_kernel, rows, width, scale, lat_axis, lat_count),
        out_shape=jax.ShapeDtypeStruct((rows, width, 128), F32),
        in_specs=[hbm, hbm] + [vmem] * 6,
        out_specs=hbm,
        scratch_shapes=[
            pltpu.VMEM((ext, 256, 128), F32),
            pltpu.VMEM((ext, wide, 128), F32),
            pltpu.VMEM((rows + 4, wide, 768), BF),
            pltpu.VMEM((ext, wide, 128), F32),
            pltpu.VMEM((768, 768), BF),
            pltpu.VMEM((256, 256), BF),
            pltpu.VMEM((rows, width, 128), F32),
            pltpu.SemaphoreType.DMA((2, ext)),
            pltpu.SemaphoreType.DMA((rows // 2,)),
        ],
        compiler_params=pltpu.CompilerParams(vmem_limit_bytes=40 << 20),
        name="tail",
    )(mixed, field, wet, table, local_weight, layer_bias.reshape(1, 128), conv_weight, conv_bias.reshape(1, 128))


def table_of(lon_ids, modes_of, parity, total_lon):
    phase = (modes_of * lon_ids + parity * (total_lon // 4)) % total_lon
    return jnp.cos(phase.astype(F32) * (2.0 * math.pi / total_lon))


def per_device(field, ocean, modes, spectral_weight, local_weight, layer_bias, conv_weight, conv_bias):
    rows, width, channels = field.shape
    lon_count = lax.axis_size(LON)
    total_lon = width * lon_count
    total_modes = modes.shape[0]
    lon_start = lax.axis_index(LON) * width
    scale = 2.0 / math.sqrt(total_modes)
    pair = jnp.repeat(modes, 2)
    parity = jnp.arange(2 * total_modes, dtype=jnp.int32) % 2
    lon_ids = (lon_start - PAD + jnp.arange(width + 2 * PAD, dtype=jnp.int32) + total_lon) % total_lon
    inverse = jnp.concatenate(stored_halves(table_of(lon_ids[:, None], pair[None], parity[None], total_lon)), 1)
    own_ids = lon_start + jnp.arange(width, dtype=jnp.int32)
    forward = table_of(own_ids[None], pair[:, None], parity[:, None], total_lon)
    partial = jnp.einsum("kj,ijc->kic", forward, field, precision=HIGH) / math.sqrt(total_lon)
    partial = partial.reshape(total_modes, 2, rows, channels).swapaxes(1, 2).reshape(total_modes, rows, 2 * channels)
    own_coeffs = sum_by_axis(partial, (("lon_0", "lon_1"), "lon_2"), 0)
    own_mixed = mix_modes(own_coeffs, spectral_weight)
    own_mixed = with_halo(own_mixed, (("lat", 1),), 1, False)
    mixed = whole_of(own_mixed, (("lon_0", "lon_1"), "lon_2"), 0)
    mixed = mixed.reshape(total_modes, rows + 2, 2, channels).swapaxes(1, 2)
    mixed = mixed.reshape(2 * total_modes, (rows + 2) * channels)
    half = rows // 2 * channels
    last = rows * channels + channels
    parts = jnp.stack([
        jnp.concatenate([mixed[:, channels : channels + half], mixed[:, last:]], 1),
        jnp.concatenate([mixed[:, channels + half : last], mixed[:, :channels]], 1),
    ])
    gap = ((0, 0), (PAD - 1, PAD - 1), (0, 0))
    edged = with_halo(field, (("lat", 0),), 1, False)
    edged = jnp.pad(with_halo(edged, ((LON, 1),), 1, True), gap)
    wet = with_halo(ocean.astype(F32)[:, :, None], (("lat", 0),), 1, False)
    wet = with_halo(wet, ((LON, 1),), 1, True)
    wet = jnp.pad(wet, gap)[:, :, 0].T
    mid = jnp.pad(wet, ((0, 0), (0, 128 - rows - 2)))
    above = jnp.pad(wet[:, :1], ((0, 0), (rows, 127 - rows)))
    below = jnp.pad(wet[:, rows + 1 :], ((0, 0), (1, 126)))
    return tail(
        parts, edged, jnp.stack([above, mid, below]), inverse, local_weight, layer_bias,
        conv_weight, conv_bias, rows, width, scale, "lat", lax.axis_size("lat"),
    )


def solution(mesh):
    split = Mesh(mesh.devices.reshape(mesh.shape["lat"], 8, 4, 2), ("lat", "lon_0", "lon_1", "lon_2"))
    placed = (P("lat", LON, None), P("lat", LON), P(), P(LON, None, None, None), P(), P(), P(), P())
    return jax.shard_map(
        per_device, mesh=split, in_specs=placed, out_specs=P("lat", LON, None), check_vma=False
    )
```

```python
import functools
import math

import jax
import jax.numpy as jnp
from jax import lax
from jax.experimental import pallas as pl
from jax.experimental.pallas import tpu as pltpu
from jax.sharding import Mesh
from jax.sharding import PartitionSpec as P

LON = ("z", "x", "core")
HIGH = lax.Precision.HIGHEST
MESH = pl.DeviceIdType.MESH
PAD = 8
BF = jnp.bfloat16
F32 = jnp.float32


def halves(value):
    high = value.astype(BF)
    return high, (value - high.astype(F32)).astype(BF)


def stored_halves(value):
    high = lax.reduce_precision(value, 8, 7)
    return high.astype(BF), (value - high).astype(BF)


def dot(a, b):
    return jnp.dot(a, b, preferred_element_type=F32)


def lane_sum(acc):
    return acc[:, :128] + acc[:, 128:]


def tail_kernel(
    rows, width, scale, lat_axis, lat_count,
    mixed_hbm, field_hbm, wet_ref, table_ref, local_ref, bias_ref, conv_ref, conv_bias_ref,
    out_hbm,
    mixed, field, hidden, mask, taps, local, out, sem_in, sem_out,
):
    ext = rows + 2
    wide = width + 2 * PAD
    half = rows // 2

    def mixed_copy(r):
        part, block = (1, half) if r == 0 else (0, half) if r == ext - 1 else divmod(r - 1, half)
        source = mixed_hbm.at[part, :, pl.ds(block * 128, 128)]
        return pltpu.make_async_copy(source, mixed.at[r], sem_in.at[0, r])

    def field_copy(r):
        return pltpu.make_async_copy(field_hbm.at[r], field.at[r], sem_in.at[1, r])

    for r in range(ext):
        mixed_copy(r).start()
        field_copy(r).start()

    high, low = halves(local_ref[...])
    both = jnp.concatenate([high, low], 1)
    local[0:128] = both
    local[128:256] = both
    for a in range(3):
        for b in range(3):
            high, low = halves(conv_ref[a, b])
            both = jnp.concatenate([high, low], 1)
            for q in range(2):
                taps[pl.ds(a * 256 + q * 128, 128), pl.ds(b * 256, 256)] = both

    lane = lax.broadcasted_iota(jnp.int32, (wide, 128), 1)
    lat = lax.axis_index(lat_axis)
    above = jnp.where(lat > 0, 1.0, 0.0).astype(F32)
    below = jnp.where(lat < lat_count - 1, 1.0, 0.0).astype(F32)
    top = pltpu.roll(wet_ref[0], 128 - rows, 1) * above
    bottom = pltpu.roll(wet_ref[2], rows, 1) * below
    wet = jnp.where(lane == 0, top, jnp.where(lane == rows + 1, bottom, wet_ref[1])).astype(BF)

    @pl.loop(0, ext)
    def _(r):
        pltpu.make_async_copy(field_hbm.at[0], field.at[0], sem_in.at[1, r]).wait()
        pltpu.make_async_copy(
            mixed_hbm.at[0, :, pl.ds(0, 128)], mixed.at[0], sem_in.at[0, r]
        ).wait()
        high, low = halves(mixed[r])
        both = jnp.concatenate([high, low], 1)
        spectral = lane_sum(dot(table_ref[...], jnp.concatenate([both, both], 0))) * scale
        high, low = halves(field[r])
        point = lane_sum(dot(jnp.concatenate([high, low], 1), local[...]))
        pick = lax.broadcasted_iota(jnp.int32, (128, 128), 0) == r
        cover = dot(wet, pick.astype(F32).astype(BF))
        mask[r] = cover
        value = cover * jax.nn.gelu(spectral + point + bias_ref[...], approximate=True)
        high, low = halves(value)
        both = jnp.concatenate([high, low], 1)
        for a in range(3):
            hidden[r + 2 - a, :, pl.ds(a * 256, 256)] = both

    group = 2

    @pl.loop(0, rows // group)
    def _(t):
        i = t * group
        block = hidden[pl.ds(i + 2, group)].reshape(group * wide, 768)
        left, middle, right = (
            lane_sum(dot(block, taps[:, pl.ds(b * 256, 256)])) for b in range(3)
        )
        total = pltpu.roll(left, 1, 0) + middle + pltpu.roll(right, group * wide - 1, 0)
        total = (total + conv_bias_ref[...]).reshape(group, wide, 128)
        total = total * mask[pl.ds(i + 1, group)]
        out[pl.ds(i, group)] = total[:, PAD : PAD + width]
        pltpu.make_async_copy(
            out.at[pl.ds(i, group)], out_hbm.at[pl.ds(i, group)], sem_out.at[t]
        ).start()

    @pl.loop(0, rows // group)
    def _(t):
        pltpu.make_async_copy(
            out.at[pl.ds(0, group)], out_hbm.at[pl.ds(0, group)], sem_out.at[t]
        ).wait()


def tail(mixed, field, wet, table, local_weight, layer_bias, conv_weight, conv_bias, rows, width, scale, lat_axis, lat_count):
    ext = rows + 2
    wide = width + 2 * PAD
    vmem = pl.BlockSpec(memory_space=pltpu.VMEM)
    hbm = pl.BlockSpec(memory_space=pl.ANY)
    return pl.pallas_call(
        functools.partial(tail_kernel, rows, width, scale, lat_axis, lat_count),
        out_shape=jax.ShapeDtypeStruct((rows, width, 128), F32),
        in_specs=[hbm, hbm] + [vmem] * 6,
        out_specs=hbm,
        scratch_shapes=[
            pltpu.VMEM((ext, 256, 128), F32),
            pltpu.VMEM((ext, wide, 128), F32),
            pltpu.VMEM((rows + 4, wide, 768), BF),
            pltpu.VMEM((ext, wide, 128), F32),
            pltpu.VMEM((768, 768), BF),
            pltpu.VMEM((256, 256), BF),
            pltpu.VMEM((rows, width, 128), F32),
            pltpu.SemaphoreType.DMA((2, ext)),
            pltpu.SemaphoreType.DMA((rows // 2,)),
        ],
        compiler_params=pltpu.CompilerParams(vmem_limit_bytes=40 << 20),
        name="tail",
    )(mixed, field, wet, table, local_weight, layer_bias.reshape(1, 128), conv_weight, conv_bias.reshape(1, 128))


def table_of(lon_ids, modes_of, parity, total_lon):
    phase = (modes_of * lon_ids + parity * (total_lon // 4)) % total_lon
    return jnp.cos(phase.astype(F32) * (2.0 * math.pi / total_lon))


def exchange_kernel(
    zs, xs, lats, scale,
    field_hbm, wet, table, weight_hbm,
    mixed_out, edged, wets,
    field, weight, sent, got, sums, half_a, half_b, full_a, full_b, part, up, down, halo, whole,
    load_sem, pair_sem, x_sem, z_sem, halo_sem, gz_sem, gx_sem, gp_sem, edge_sem, local_sem,
):
    rows, width, _ = field.shape
    half = rows // 2
    lanes = half * 128
    cut = lanes // 2
    lat, z, x, core = (lax.axis_index(name) for name in ("lat", "z", "x", "core"))
    other = 1 - core

    def wrap(value, size):
        return lax.rem(value + size, size)

    def device(lat=lat, z=z, x=x, core=core):
        return {"lat": lat, "z": z, "x": x, "core": core}

    def lon_at(step):
        spot = wrap((z * xs + x) * 2 + core + step, zs * xs * 2)
        return {"z": lax.div(spot, 2 * xs), "x": lax.rem(lax.div(spot, 2), xs), "core": lax.rem(spot, 2)}

    right, left, across = wrap(x + 1, xs), wrap(x - 1, xs), wrap(x + 2, xs)
    higher, lower = wrap(z + 1, zs), wrap(z - 1, zs)
    south, north = wrap(lat + 1, lats), wrap(lat - 1, lats)
    east, west = lon_at(1), lon_at(-1)

    for i in range(rows):
        pltpu.make_async_copy(field_hbm.at[i], field.at[i], load_sem.at[i]).start()
    own_weight = pltpu.make_async_copy(weight_hbm, weight.at[core], local_sem.at[0])
    own_weight.start()

    barrier = pltpu.get_barrier_semaphore()
    friends = [
        device(core=other), device(x=right), device(x=left), device(z=higher), device(z=lower),
        device(lat=south), device(lat=north), device(**east), device(**west),
        device(lat=south, **east), device(lat=south, **west),
        device(lat=north, **east), device(lat=north, **west),
    ]
    for friend in friends:
        pl.semaphore_signal(barrier, inc=1, device_id=friend, device_id_type=MESH)

    pending = []

    def send(source, target, sems, index, where):
        copy = pltpu.make_async_remote_copy(
            src_ref=source, dst_ref=target, send_sem=sems.at[0, index], recv_sem=sems.at[1, index],
            device_id=where, device_id_type=MESH,
        )
        copy.start()
        pending.append(copy)
        return copy

    def coefficients(first):
        pltpu.make_async_copy(field_hbm.at[0], field.at[0], load_sem.at[first]).wait()
        pltpu.make_async_copy(field_hbm.at[0], field.at[0], load_sem.at[first + 1]).wait()
        high, low = halves(jnp.concatenate([field[first], field[first + 1]], 1))
        result = dot(table[...], jnp.concatenate([high, high], 0)) + dot(table[:, :width], low)
        return result * scale

    pairs = half // 2
    pair_copies = []
    for p in range(pairs):
        sent[p] = coefficients(other * half + 2 * p)
        if p == 0:
            pl.semaphore_wait(barrier, len(friends))
        pair_copies.append(send(sent.at[p], got.at[p], pair_sem, p, device(core=other)))
    weight_copy = send(weight_hbm, weight.at[core], halo_sem, 1, device(core=other))

    edges = []

    def edge(source, target, where):
        edges.append(send(source, target, edge_sem, len(edges), where))

    edge(field_hbm.at[rows - 1], edged.at[0, pl.ds(PAD, width)], device(lat=south))
    edge(field_hbm.at[0], edged.at[rows + 1, pl.ds(PAD, width)], device(lat=north))
    edge(wet, wets.at[0, pl.ds(PAD, width)], device(lat=south))
    edge(wet, wets.at[2, pl.ds(PAD, width)], device(lat=north))

    for p in range(pairs):
        mine = coefficients(core * half + 2 * p)
        pair_copies[p].wait_recv()
        mine = mine + got[p]
        sums[:, :, :, pl.ds(p * 256, 256)] = mine.reshape(zs, xs, 8, 256)

    order = (4, 3, 5, 2, 6, 1, 7, 0)
    slices = [wrap(z + step, zs) for step in order]
    low_lanes, high_lanes = pl.ds(0, cut), pl.ds(cut, cut)
    firsts = []
    for n, zz in enumerate(slices):
        firsts.append((
            send(sums.at[zz, across, :, low_lanes], half_a.at[n], x_sem, n, device(x=right)),
            send(sums.at[zz, across, :, high_lanes], half_b.at[n], x_sem, 8 + n, device(x=left)),
        ))
    seconds = []
    for n, zz in enumerate(slices):
        firsts[n][0].wait_recv()
        sums[zz, right, :, low_lanes] = sums[zz, right, :, low_lanes] + half_a[n]
        to_right = send(sums.at[zz, right], full_a.at[n], x_sem, 16 + n, device(x=right))
        firsts[n][1].wait_recv()
        sums[zz, left, :, high_lanes] = sums[zz, left, :, high_lanes] + half_b[n]
        to_left = send(sums.at[zz, left], full_b.at[n], x_sem, 24 + n, device(x=left))
        seconds.append((to_right, to_left))

    last = width - PAD
    middle, ends = pl.ds(1, rows), (pl.ds(0, PAD), pl.ds(last, PAD))
    outer = (pl.ds(PAD + width, PAD), pl.ds(0, PAD))

    def send_edges():
        for side, lon in ((0, west), (1, east)):
            edge(field_hbm.at[:, ends[side]], edged.at[middle, outer[side]], device(**lon))
            edge(wet.at[ends[side]], wets.at[1, outer[side]], device(**lon))
            edge(field_hbm.at[rows - 1, ends[side]], edged.at[0, outer[side]], device(lat=south, **lon))
            edge(wet.at[ends[side]], wets.at[0, outer[side]], device(lat=south, **lon))
            edge(field_hbm.at[0, ends[side]], edged.at[rows + 1, outer[side]], device(lat=north, **lon))
            edge(wet.at[ends[side]], wets.at[2, outer[side]], device(lat=north, **lon))

    rising, falling = [], []
    for n, zz in enumerate(slices):
        seconds[n][0].wait_recv()
        seconds[n][1].wait_recv()
        total = sums[zz, x] + full_a[n] + full_b[n]
        step = (n - 1) // 2
        if n == 0:
            part[n] = total
            rising.append(send(part.at[n, :, low_lanes], up.at[0, :, low_lanes], z_sem, 0, device(z=higher)))
            falling.append(send(part.at[n, :, high_lanes], down.at[0, :, high_lanes], z_sem, 4, device(z=lower)))
            send_edges()
        elif n == 7:
            rising[3].wait_recv()
            falling[3].wait_recv()
            total = total + up[3] + down[3]
        else:
            rises = n % 2 == 1
            chain, buffer = (rising, up) if rises else (falling, down)
            chain[step].wait_recv()
            if step == 0:
                span = low_lanes if rises else high_lanes
                part[n] = total
                part[n, :, span] = part[n, :, span] + buffer[0, :, span]
            else:
                part[n] = total + buffer[step]
            chain.append(send(
                part.at[n], buffer.at[step + 1], z_sem, (0 if rises else 4) + step + 1,
                device(z=higher if rises else lower),
            ))

    own_weight.wait()
    weight_copy.wait_recv()
    terms = jnp.concatenate([total[:, i * 128 : (i + 1) * 128] for i in range(half)], 0)
    spot = lax.rem(lax.broadcasted_iota(jnp.int32, (half * 8, 128), 0), 8)
    real, imag = jnp.zeros((half * 8, 128), F32), jnp.zeros((half * 8, 128), F32)
    for m in range(4):
        chosen = (spot == 2 * m) | (spot == 2 * m + 1)
        picked = jnp.where(chosen, terms, 0.0)
        real = real + jnp.dot(picked, weight[m // 2, m % 2, 0], precision=HIGH, preferred_element_type=F32)
        imag = imag + jnp.dot(picked, weight[m // 2, m % 2, 1], precision=HIGH, preferred_element_type=F32)
    even = lax.rem(spot, 2) == 0
    mixed = real + jnp.where(even, -pltpu.roll(imag, half * 8 - 1, 0), pltpu.roll(imag, 1, 0))
    for i in range(half):
        whole[z, x, :, pl.ds(i * 128, 128)] = mixed[i * 8 : (i + 1) * 8]
    halo[...] = jnp.where(core == 0, mixed[:8], mixed[(half - 1) * 8 :])
    tail_lanes = pl.ds(lanes, 128)
    row_copy = send(halo, whole.at[z, x, :, tail_lanes], halo_sem, 0, device(lat=wrap(lat - 1 + 2 * core, lats)))
    row_copy.wait_recv()

    front, back = pl.ds(0, cut), pl.ds(cut, lanes + 128 - cut)
    order = (0, 7, 1, 6, 2, 5, 3, 4)
    slices = [wrap(z + step, zs) for step in order]
    rising, falling, sideways, relays, locals_, gathered = [], [], [], [], [], []

    def spread(n):
        zz = slices[n]
        mine = whole.at[zz, x]
        sideways.append((
            send(mine, mine, gx_sem, n, device(x=right)),
            send(mine, mine, gx_sem, 8 + n, device(x=left)),
        ))

    def relay(n):
        zz = slices[n]
        sideways[n][0].wait_recv()
        from_left = whole.at[zz, left, :, front]
        first = send(from_left, from_left, gx_sem, 16 + n, device(x=right))
        sideways[n][1].wait_recv()
        from_right = whole.at[zz, right, :, back]
        second = send(from_right, from_right, gx_sem, 24 + n, device(x=left))
        relays.append((first, second))

    def finish(n):
        zz = slices[n]
        relays[n][0].wait_recv()
        relays[n][1].wait_recv()
        gathered.append(send(whole.at[zz], mixed_out.at[core, zz], gp_sem, n, device(core=other)))
        kept = pltpu.make_async_copy(whole.at[zz], mixed_out.at[core, zz], local_sem.at[3 + n])
        kept.start()
        locals_.append(kept)

    def climb(zz, step):
        source = whole.at[zz, x] if step < 3 else whole.at[zz, x, :, front]
        rising.append(send(source, source, gz_sem, step, device(z=higher)))

    def descend(zz, step):
        source = whole.at[zz, x] if step < 3 else whole.at[zz, x, :, back]
        falling.append(send(source, source, gz_sem, 4 + step, device(z=lower)))

    climb(slices[0], 0)
    descend(slices[0], 0)
    spread(0)
    for n in range(1, 8):
        step = (n - 1) // 2
        if n == 7:
            rising[3].wait_recv()
            falling[3].wait_recv()
        elif n % 2 == 1:
            rising[step].wait_recv()
            climb(slices[n], step + 1)
        else:
            falling[step].wait_recv()
            descend(slices[n], step + 1)
        spread(n)
        relay(n - 1)
        if n >= 2:
            finish(n - 2)
    relay(7)
    finish(6)
    finish(7)

    inner = pltpu.make_async_copy(field, edged.at[middle, pl.ds(PAD, width)], local_sem.at[1])
    inner.start()
    inner_wet = pltpu.make_async_copy(wet, wets.at[1, pl.ds(PAD, width)], local_sem.at[2])
    inner_wet.start()
    for copy in edges + gathered:
        copy.wait_recv()
    for copy in pending:
        copy.wait_send()
    for copy in locals_ + [inner, inner_wet]:
        copy.wait()


def exchange(field, wet, table, weight, lats, zs, xs, scale):
    rows, width, _ = field.shape
    wide = width + 2 * PAD
    lanes = rows // 2 * 128
    vmem = pl.BlockSpec(memory_space=pltpu.VMEM)
    hbm = pl.BlockSpec(memory_space=pl.ANY)
    dma = pltpu.SemaphoreType.DMA
    return pl.pallas_call(
        functools.partial(exchange_kernel, zs, xs, lats, scale),
        out_shape=(
            jax.ShapeDtypeStruct((2, zs, xs, 8, lanes + 128), F32),
            jax.ShapeDtypeStruct((rows + 2, wide, 128), F32),
            jax.ShapeDtypeStruct((3, wide, 128), F32),
        ),
        in_specs=[hbm, vmem, vmem, hbm],
        out_specs=(hbm, hbm, hbm),
        scratch_shapes=[
            pltpu.VMEM((rows, width, 128), F32),
            pltpu.VMEM((2, *weight.shape), F32),
            pltpu.VMEM((rows // 4, 256, 256), F32),
            pltpu.VMEM((rows // 4, 256, 256), F32),
            pltpu.VMEM((zs, xs, 8, lanes), F32),
            pltpu.VMEM((zs, 8, lanes // 2), F32),
            pltpu.VMEM((zs, 8, lanes // 2), F32),
            pltpu.VMEM((zs, 8, lanes), F32),
            pltpu.VMEM((zs, 8, lanes), F32),
            pltpu.VMEM((zs, 8, lanes), F32),
            pltpu.VMEM((4, 8, lanes), F32),
            pltpu.VMEM((4, 8, lanes), F32),
            pltpu.VMEM((8, 128), F32),
            pltpu.VMEM((zs, xs, 8, lanes + 128), F32),
            dma((rows,)), dma((2, 4)), dma((2, 32)), dma((2, 8)), dma((2, 2)), dma((2, 8)),
            dma((2, 32)), dma((2, 8)), dma((2, 16)), dma((11,)),
        ],
        compiler_params=pltpu.CompilerParams(
            collective_id=0, has_side_effects=True, vmem_limit_bytes=32 << 20
        ),
        name="exchange",
    )(field, wet, table, weight)


def per_device(field, ocean, modes, spectral_weight, local_weight, layer_bias, conv_weight, conv_bias):
    rows, width, channels = field.shape
    lats, zs, xs = (lax.axis_size(name) for name in ("lat", "z", "x"))
    total_lon = width * zs * xs * 2
    total_modes = modes.shape[0]
    lon_start = lax.axis_index(LON) * width
    pair = jnp.repeat(modes, 2)
    parity = jnp.arange(2 * total_modes, dtype=jnp.int32) % 2
    own_ids = lon_start + jnp.arange(width, dtype=jnp.int32)
    forward = jnp.concatenate(stored_halves(table_of(own_ids[None], pair[:, None], parity[:, None], total_lon)), 1)
    wet = jnp.pad(ocean.astype(F32).T, ((0, 0), (1, 127 - rows)))
    mixed, edged, wets = exchange(
        field, wet, forward, spectral_weight, lats, zs, xs, 1.0 / math.sqrt(total_lon)
    )
    lon_ids = (lon_start - PAD + jnp.arange(width + 2 * PAD, dtype=jnp.int32) + total_lon) % total_lon
    inverse = jnp.concatenate(stored_halves(table_of(lon_ids[:, None], pair[None], parity[None], total_lon)), 1)
    mixed = mixed.reshape(2, 2 * total_modes, -1)
    return tail(
        mixed, edged, wets, inverse, local_weight, layer_bias,
        conv_weight, conv_bias, rows, width, 2.0 / math.sqrt(total_modes), "lat", lats,
    )


def solution(mesh):
    split = Mesh(mesh.devices.reshape(mesh.shape["lat"], 8, 4, 2), ("lat", *LON))
    placed = (P("lat", LON, None), P("lat", LON), P(), P(LON, None, None, None), P(), P(), P(), P())
    return jax.shard_map(
        per_device, mesh=split, in_specs=placed, out_specs=P("lat", LON, None), check_vma=False
    )
```

```python
import functools
import math

import jax
import jax.numpy as jnp
from jax import lax
from jax.experimental import pallas as pl
from jax.experimental.pallas import tpu as pltpu
from jax.sharding import Mesh
from jax.sharding import PartitionSpec as P

LON = ("z", "x", "core")
HIGH = lax.Precision.HIGHEST
MESH = pl.DeviceIdType.MESH
PAD = 8
BF = jnp.bfloat16
F32 = jnp.float32


def halves(value):
    high = value.astype(BF)
    return high, (value - high.astype(F32)).astype(BF)


def dot(a, b):
    return jnp.dot(a, b, preferred_element_type=F32)


def lane_sum(acc):
    return acc[:, :128] + acc[:, 128:]


def tail_kernel(
    rows, width, scale, lat_axis, lat_count,
    mixed, field, wet_ref, table_ref, local_ref, bias_ref, conv_ref, conv_bias_ref,
    out_hbm,
    hidden, mask, taps, local, out, sem_out,
):
    ext = rows + 2
    wide = width + 2 * PAD
    half = rows // 2

    high, low = halves(local_ref[...])
    both = jnp.concatenate([high, low], 1)
    local[0:128] = both
    local[128:256] = both
    for a in range(3):
        for b in range(3):
            high, low = halves(conv_ref[a, b])
            both = jnp.concatenate([high, low], 1)
            for q in range(2):
                taps[pl.ds(a * 256 + q * 128, 128), pl.ds(b * 256, 256)] = both

    lane = lax.broadcasted_iota(jnp.int32, (wide, 128), 1)
    lat = lax.axis_index(lat_axis)
    above = jnp.where(lat > 0, 1.0, 0.0).astype(F32)
    below = jnp.where(lat < lat_count - 1, 1.0, 0.0).astype(F32)
    top = pltpu.roll(wet_ref[0], 128 - rows, 1) * above
    bottom = pltpu.roll(wet_ref[2], rows, 1) * below
    wet = jnp.where(lane == 0, top, jnp.where(lane == rows + 1, bottom, wet_ref[1])).astype(BF)

    @pl.loop(0, ext)
    def _(r):
        outer = (r == 0) | (r == ext - 1)
        second = (r > half) & (r < ext - 1) | (r == 0)
        block = jnp.where(outer, half, lax.rem(r + half - 1, half))
        spot = pl.ds(pl.multiple_of(block * 128, 128), 128)
        high, low = halves(mixed[jnp.where(second, 1, 0), :, spot])
        both = jnp.concatenate([high, low], 1)
        spectral = lane_sum(dot(table_ref[...], jnp.concatenate([both, both], 0))) * scale
        high, low = halves(field[r])
        point = lane_sum(dot(jnp.concatenate([high, low], 1), local[...]))
        pick = lax.broadcasted_iota(jnp.int32, (128, 128), 0) == r
        cover = dot(wet, pick.astype(F32).astype(BF))
        mask[r] = cover
        value = cover * jax.nn.gelu(spectral + point + bias_ref[...], approximate=True)
        high, low = halves(value)
        both = jnp.concatenate([high, low], 1)
        for a in range(3):
            hidden[r + 2 - a, :, pl.ds(a * 256, 256)] = both

    group = 2

    @pl.loop(0, rows // group)
    def _(t):
        i = t * group
        block = hidden[pl.ds(i + 2, group)].reshape(group * wide, 768)
        left, middle, right = (
            lane_sum(dot(block, taps[:, pl.ds(b * 256, 256)])) for b in range(3)
        )
        total = pltpu.roll(left, 1, 0) + middle + pltpu.roll(right, group * wide - 1, 0)
        total = (total + conv_bias_ref[...]).reshape(group, wide, 128)
        total = total * mask[pl.ds(i + 1, group)]
        out[pl.ds(i, group)] = total[:, PAD : PAD + width]
        pltpu.make_async_copy(
            out.at[pl.ds(i, group)], out_hbm.at[pl.ds(i, group)], sem_out.at[t]
        ).start()

    @pl.loop(0, rows // group)
    def _(t):
        pltpu.make_async_copy(
            out.at[pl.ds(0, group)], out_hbm.at[pl.ds(0, group)], sem_out.at[t]
        ).wait()


def tail(mixed, field, wet, table, local_weight, layer_bias, conv_weight, conv_bias, rows, width, scale, lat_axis, lat_count):
    ext = rows + 2
    wide = width + 2 * PAD
    vmem = pl.BlockSpec(memory_space=pltpu.VMEM)
    hbm = pl.BlockSpec(memory_space=pl.ANY)
    return pl.pallas_call(
        functools.partial(tail_kernel, rows, width, scale, lat_axis, lat_count),
        out_shape=jax.ShapeDtypeStruct((rows, width, 128), F32),
        in_specs=[vmem] * 8,
        out_specs=hbm,
        scratch_shapes=[
            pltpu.VMEM((rows + 4, wide, 768), BF),
            pltpu.VMEM((ext, wide, 128), F32),
            pltpu.VMEM((768, 768), BF),
            pltpu.VMEM((256, 256), BF),
            pltpu.VMEM((rows, width, 128), F32),
            pltpu.SemaphoreType.DMA((rows // 2,)),
        ],
        compiler_params=pltpu.CompilerParams(vmem_limit_bytes=40 << 20),
        name="tail",
    )(mixed, field, wet, table, local_weight, layer_bias.reshape(1, 128), conv_weight, conv_bias.reshape(1, 128))


def exchange_kernel(
    zs, xs, lats, scale,
    field_hbm, ocean_hbm, modes_hbm, weight_hbm,
    mixed_out, edged, wets, table_out,
    ocean, modes, wet, table, turned, field, weight, sent, got, sums, half_a, half_b, full_a, full_b, part, up, down, halo, whole,
    load_sem, pair_sem, x_sem, z_sem, halo_sem, gz_sem, gx_sem, gp_sem, edge_sem, local_sem,
):
    rows, width, _ = field.shape
    half = rows // 2
    lanes = half * 128
    cut = lanes // 2
    wide = width + 2 * PAD
    total_lon = zs * xs * 2 * width
    lat, z, x, core = (lax.axis_index(name) for name in ("lat", "z", "x", "core"))
    other = 1 - core

    def wrap(value, size):
        return lax.rem(value + size, size)

    def device(lat=lat, z=z, x=x, core=core):
        return {"lat": lat, "z": z, "x": x, "core": core}

    def lon_at(step):
        spot = wrap((z * xs + x) * 2 + core + step, zs * xs * 2)
        return {"z": lax.div(spot, 2 * xs), "x": lax.rem(lax.div(spot, 2), xs), "core": lax.rem(spot, 2)}

    right, left, across = wrap(x + 1, xs), wrap(x - 1, xs), wrap(x + 2, xs)
    higher, lower = wrap(z + 1, zs), wrap(z - 1, zs)
    south, north = wrap(lat + 1, lats), wrap(lat - 1, lats)
    east, west = lon_at(1), lon_at(-1)

    small = [
        pltpu.make_async_copy(modes_hbm, modes, local_sem.at[12]),
        pltpu.make_async_copy(ocean_hbm, ocean, local_sem.at[13]),
    ]
    for copy in small:
        copy.start()
    for i in range(rows):
        row = (other if i < half else core) * half + i % half
        pltpu.make_async_copy(field_hbm.at[row], field.at[row], load_sem.at[row]).start()
    own_weight = pltpu.make_async_copy(weight_hbm, weight.at[core], local_sem.at[0])
    own_weight.start()

    barrier = pltpu.get_barrier_semaphore()
    beyond, behind = wrap(z + 2, zs), wrap(z - 2, zs)
    friends = [
        device(core=other), device(x=right), device(x=left), device(z=higher), device(z=lower),
        device(z=beyond), device(z=behind), device(lat=south), device(lat=north),
        device(**east), device(**west),
    ]
    for friend in friends:
        pl.semaphore_signal(barrier, inc=1, device_id=friend, device_id_type=MESH)

    for copy in small:
        copy.wait()
    count = 2 * modes.shape[1]
    slot = lax.broadcasted_iota(jnp.int32, (count // 2, count), 1)
    spread_out = lax.div(slot, 2) == lax.broadcasted_iota(jnp.int32, (count // 2, count), 0)
    pair = jnp.dot(
        jnp.broadcast_to(modes[...].astype(F32), (8, count // 2)), spread_out.astype(F32),
        precision=HIGH, preferred_element_type=F32,
    )[:1].astype(jnp.int32)
    start = ((z * xs + x) * 2 + core) * width - PAD + total_lon
    lon = start + lax.broadcasted_iota(jnp.int32, (wide, count), 0)
    odd = lax.broadcasted_iota(jnp.int32, (wide, count), 1) & 1
    phase = (pair * (lon & (total_lon - 1)) + odd * (total_lon // 4)) & (total_lon - 1)
    wave = jnp.cos(phase.astype(F32) * (2.0 * math.pi / total_lon))
    high, low = halves(wave)
    turned[:, :count] = high
    turned[:, count:] = low
    high, low = halves(wave[PAD : PAD + width].T)
    table[:, :width] = high
    table[:, width:] = low
    dry = jnp.zeros((128 - rows, width), F32)
    wet[...] = pltpu.roll(jnp.concatenate([ocean[...].astype(F32), dry], 0).T, 1, 1)

    pending = []

    def send(source, target, sems, index, where):
        copy = pltpu.make_async_remote_copy(
            src_ref=source, dst_ref=target, send_sem=sems.at[0, index], recv_sem=sems.at[1, index],
            device_id=where, device_id_type=MESH,
        )
        copy.start()
        pending.append(copy)
        return copy

    def coefficients(first):
        pltpu.make_async_copy(field_hbm.at[0], field.at[0], load_sem.at[first]).wait()
        pltpu.make_async_copy(field_hbm.at[0], field.at[0], load_sem.at[first + 1]).wait()
        high, low = halves(jnp.concatenate([field[first], field[first + 1]], 1))
        result = dot(table[...], jnp.concatenate([high, high], 0)) + dot(table[:, :width], low)
        return result * scale

    pairs = half // 2
    pair_copies = []
    for p in range(pairs):
        sent[p] = coefficients(other * half + 2 * p)
        if p == 0:
            pl.semaphore_wait(barrier, len(friends))
        pair_copies.append(send(sent.at[p], got.at[p], pair_sem, p, device(core=other)))
    weight_copy = send(weight_hbm, weight.at[core], halo_sem, 1, device(core=other))

    edges = []

    def edge(source, target, where):
        edges.append(send(source, target, edge_sem, len(edges), where))

    edge(field_hbm.at[rows - 1], edged.at[0, pl.ds(PAD, width)], device(lat=south))
    edge(field_hbm.at[0], edged.at[rows + 1, pl.ds(PAD, width)], device(lat=north))
    edge(wet, wets.at[0, pl.ds(PAD, width)], device(lat=south))
    edge(wet, wets.at[2, pl.ds(PAD, width)], device(lat=north))

    for p in range(pairs):
        mine = coefficients(core * half + 2 * p)
        pair_copies[p].wait_recv()
        mine = mine + got[p]
        sums[:, :, :, pl.ds(p * 256, 256)] = mine.reshape(zs, xs, 8, 256)

    middle = pl.ds(PAD, width)
    inner = [
        pltpu.make_async_copy(field, edged.at[pl.ds(1, rows), middle], local_sem.at[1]),
        pltpu.make_async_copy(wet, wets.at[1, middle], local_sem.at[2]),
    ]
    kept_table = pltpu.make_async_copy(turned, table_out, local_sem.at[11])
    for copy in inner + [kept_table]:
        copy.start()

    order = (4, 3, 5, 2, 6, 1, 7, 0)
    slices = [wrap(z + step, zs) for step in order]
    low_lanes, high_lanes = pl.ds(0, cut), pl.ds(cut, cut)
    firsts = []
    for n, zz in enumerate(slices):
        firsts.append((
            send(sums.at[zz, across, :, low_lanes], half_a.at[n], x_sem, n, device(x=right)),
            send(sums.at[zz, across, :, high_lanes], half_b.at[n], x_sem, 8 + n, device(x=left)),
        ))
    seconds = []
    for n, zz in enumerate(slices):
        firsts[n][0].wait_recv()
        sums[zz, right, :, low_lanes] = sums[zz, right, :, low_lanes] + half_a[n]
        to_right = send(sums.at[zz, right], full_a.at[n], x_sem, 16 + n, device(x=right))
        firsts[n][1].wait_recv()
        sums[zz, left, :, high_lanes] = sums[zz, left, :, high_lanes] + half_b[n]
        to_left = send(sums.at[zz, left], full_b.at[n], x_sem, 24 + n, device(x=left))
        seconds.append((to_right, to_left))

    def send_edges():
        for copy in edges:
            copy.wait_recv()
        for copy in inner:
            copy.wait()
        for source, target, lon in ((PAD, PAD + width, west), (width, 0, east)):
            edge(edged.at[:, pl.ds(source, PAD)], edged.at[:, pl.ds(target, PAD)], device(**lon))
            edge(wets.at[:, pl.ds(source, PAD)], wets.at[:, pl.ds(target, PAD)], device(**lon))

    rising, falling = [], []
    for n, zz in enumerate(slices):
        seconds[n][0].wait_recv()
        seconds[n][1].wait_recv()
        total = sums[zz, x] + full_a[n] + full_b[n]
        step = (n - 1) // 2
        if n == 0:
            part[n] = total
            rising.append(send(part.at[n, :, low_lanes], up.at[0, :, low_lanes], z_sem, 0, device(z=higher)))
            falling.append(send(part.at[n, :, high_lanes], down.at[0, :, high_lanes], z_sem, 4, device(z=lower)))
            send_edges()
        elif n == 7:
            rising[3].wait_recv()
            falling[3].wait_recv()
            total = total + up[3] + down[3]
        else:
            rises = n % 2 == 1
            chain, buffer = (rising, up) if rises else (falling, down)
            chain[step].wait_recv()
            if step == 0:
                span = low_lanes if rises else high_lanes
                part[n] = total
                part[n, :, span] = part[n, :, span] + buffer[0, :, span]
            else:
                part[n] = total + buffer[step]
            chain.append(send(
                part.at[n], buffer.at[step + 1], z_sem, (0 if rises else 4) + step + 1,
                device(z=higher if rises else lower),
            ))

    own_weight.wait()
    weight_copy.wait_recv()
    terms = jnp.concatenate([total[:, i * 128 : (i + 1) * 128] for i in range(half)], 0)
    spot = lax.rem(lax.broadcasted_iota(jnp.int32, (half * 8, 128), 0), 8)
    real, imag = jnp.zeros((half * 8, 128), F32), jnp.zeros((half * 8, 128), F32)
    for m in range(4):
        chosen = (spot == 2 * m) | (spot == 2 * m + 1)
        picked = jnp.where(chosen, terms, 0.0)
        real = real + jnp.dot(picked, weight[m // 2, m % 2, 0], precision=HIGH, preferred_element_type=F32)
        imag = imag + jnp.dot(picked, weight[m // 2, m % 2, 1], precision=HIGH, preferred_element_type=F32)
    even = lax.rem(spot, 2) == 0
    mixed = real + jnp.where(even, -pltpu.roll(imag, half * 8 - 1, 0), pltpu.roll(imag, 1, 0))
    for i in range(half):
        whole[z, x, :, pl.ds(i * 128, 128)] = mixed[i * 8 : (i + 1) * 8]
    halo[...] = jnp.where(core == 0, mixed[:8], mixed[(half - 1) * 8 :])
    tail_lanes = pl.ds(lanes, 128)
    row_copy = send(halo, whole.at[z, x, :, tail_lanes], halo_sem, 0, device(lat=wrap(lat - 1 + 2 * core, lats)))
    row_copy.wait_recv()

    front, back = pl.ds(0, cut), pl.ds(cut, lanes + 128 - cut)
    order = (0, 7, 1, 6, 2, 5, 3, 4)
    slices = [wrap(z + step, zs) for step in order]
    sideways, relays, locals_, gathered = [], [], [], []

    def spread(n):
        zz = slices[n]
        mine = whole.at[zz, x]
        sideways.append((
            send(mine, mine, gx_sem, n, device(x=right)),
            send(mine, mine, gx_sem, 8 + n, device(x=left)),
        ))

    def relay(n):
        zz = slices[n]
        sideways[n][0].wait_recv()
        from_left = whole.at[zz, left, :, front]
        first = send(from_left, from_left, gx_sem, 16 + n, device(x=right))
        sideways[n][1].wait_recv()
        from_right = whole.at[zz, right, :, back]
        second = send(from_right, from_right, gx_sem, 24 + n, device(x=left))
        relays.append((first, second))

    def finish(n):
        zz = slices[n]
        relays[n][0].wait_recv()
        relays[n][1].wait_recv()
        gathered.append(send(whole.at[zz], mixed_out.at[core, zz], gp_sem, n, device(core=other)))
        kept = pltpu.make_async_copy(whole.at[zz], mixed_out.at[core, zz], local_sem.at[3 + n])
        kept.start()
        locals_.append(kept)

    def along(n, where, index, span=None):
        source = whole.at[slices[n], x] if span is None else whole.at[slices[n], x, :, span]
        return send(source, source, gz_sem, index, device(z=where))

    far_up, far_down = along(0, beyond, 2), along(0, behind, 3)
    near_up, near_down = along(0, higher, 0), along(0, lower, 1)
    spread(0)
    near_up.wait_recv()
    spread(1)
    near_down.wait_recv()
    spread(2)
    far_up.wait_recv()
    next_up, half_up = along(3, higher, 4), along(3, beyond, 6, front)
    far_down.wait_recv()
    next_down, half_down = along(4, lower, 5), along(4, behind, 7, back)
    spread(3)
    spread(4)
    for n in range(3):
        relay(n)
    next_up.wait_recv()
    spread(5)
    next_down.wait_recv()
    spread(6)
    half_up.wait_recv()
    half_down.wait_recv()
    spread(7)
    finish(0)
    for n in range(3, 8):
        relay(n)
        finish(n - 2)
    finish(6)
    finish(7)

    for copy in edges[4:] + gathered:
        copy.wait_recv()
    for copy in pending:
        copy.wait_send()
    for copy in locals_ + [kept_table]:
        copy.wait()


def exchange(field, ocean, modes, weight, lats, zs, xs, scale):
    rows, width, _ = field.shape
    wide = width + 2 * PAD
    lanes = rows // 2 * 128
    hbm = pl.BlockSpec(memory_space=pl.ANY)
    dma = pltpu.SemaphoreType.DMA
    return pl.pallas_call(
        functools.partial(exchange_kernel, zs, xs, lats, scale),
        out_shape=(
            jax.ShapeDtypeStruct((2, zs, xs, 8, lanes + 128), F32),
            jax.ShapeDtypeStruct((rows + 2, wide, 128), F32),
            jax.ShapeDtypeStruct((3, wide, 128), F32),
            jax.ShapeDtypeStruct((wide, 512), BF),
        ),
        in_specs=[hbm] * 4,
        out_specs=(hbm, hbm, hbm, hbm),
        scratch_shapes=[
            pltpu.VMEM(ocean.shape, jnp.int32),
            pltpu.VMEM((1, modes.size), jnp.int32),
            pltpu.VMEM((width, 128), F32),
            pltpu.VMEM((256, 2 * width), BF),
            pltpu.VMEM((wide, 512), BF),
            pltpu.VMEM((rows, width, 128), F32),
            pltpu.VMEM((2, *weight.shape), F32),
            pltpu.VMEM((rows // 4, 256, 256), F32),
            pltpu.VMEM((rows // 4, 256, 256), F32),
            pltpu.VMEM((zs, xs, 8, lanes), F32),
            pltpu.VMEM((zs, 8, lanes // 2), F32),
            pltpu.VMEM((zs, 8, lanes // 2), F32),
            pltpu.VMEM((zs, 8, lanes), F32),
            pltpu.VMEM((zs, 8, lanes), F32),
            pltpu.VMEM((zs, 8, lanes), F32),
            pltpu.VMEM((4, 8, lanes), F32),
            pltpu.VMEM((4, 8, lanes), F32),
            pltpu.VMEM((8, 128), F32),
            pltpu.VMEM((zs, xs, 8, lanes + 128), F32),
            dma((rows,)), dma((2, 4)), dma((2, 32)), dma((2, 8)), dma((2, 2)), dma((2, 8)),
            dma((2, 32)), dma((2, 8)), dma((2, 8)), dma((14,)),
        ],
        compiler_params=pltpu.CompilerParams(
            collective_id=0, has_side_effects=True, vmem_limit_bytes=32 << 20
        ),
        name="exchange",
    )(*(pltpu.with_memory_space_constraint(a, pltpu.HBM) for a in (field, ocean, modes.reshape(1, -1), weight)))


def per_device(field, ocean, modes, spectral_weight, local_weight, layer_bias, conv_weight, conv_bias):
    rows, width, channels = field.shape
    lats, zs, xs = (lax.axis_size(name) for name in ("lat", "z", "x"))
    total_lon = width * zs * xs * 2
    total_modes = modes.shape[0]
    mixed, edged, wets, inverse = exchange(
        field, ocean, modes, spectral_weight, lats, zs, xs, 1.0 / math.sqrt(total_lon)
    )
    mixed = mixed.reshape(2, 2 * total_modes, -1)
    return tail(
        mixed, edged, wets, inverse, local_weight, layer_bias,
        conv_weight, conv_bias, rows, width, 2.0 / math.sqrt(total_modes), "lat", lats,
    )


def solution(mesh):
    split = Mesh(mesh.devices.reshape(mesh.shape["lat"], 8, 4, 2), ("lat", *LON))
    placed = (P("lat", LON, None), P("lat", LON), P(), P(LON, None, None, None), P(), P(), P(), P())
    return jax.shard_map(
        per_device, mesh=split, in_specs=placed, out_specs=P("lat", LON, None), check_vma=False
    )
```

```python
import functools
import math

import jax
import jax.numpy as jnp
from jax import lax
from jax.experimental import pallas as pl
from jax.experimental.pallas import tpu as pltpu
from jax.sharding import Mesh
from jax.sharding import PartitionSpec as P

LON = ("z", "x", "core")
HIGH = lax.Precision.HIGHEST
MESH = pl.DeviceIdType.MESH
PAD = 8
BF = jnp.bfloat16
F32 = jnp.float32


def halves(value):
    high = value.astype(BF)
    return high, (value - high.astype(F32)).astype(BF)


def dot(a, b):
    return jnp.dot(a, b, preferred_element_type=F32)


def lane_sum(acc):
    return acc[:, :128] + acc[:, 128:]


def tail_kernel(
    rows, width, scale, lat_axis, lat_count,
    mixed, field, wet_ref, table_ref, local_ref, bias_ref, conv_ref, conv_bias_ref,
    out_hbm,
    hidden, mask, taps, local, out, sem_out,
):
    ext = rows + 2
    wide = width + 2 * PAD
    half = rows // 2

    high, low = halves(local_ref[...])
    both = jnp.concatenate([high, low], 1)
    local[0:128] = both
    local[128:256] = both
    for a in range(3):
        for b in range(3):
            high, low = halves(conv_ref[a, b])
            both = jnp.concatenate([high, low], 1)
            for q in range(2):
                taps[pl.ds(a * 256 + q * 128, 128), pl.ds(b * 256, 256)] = both

    lane = lax.broadcasted_iota(jnp.int32, (wide, 128), 1)
    lat = lax.axis_index(lat_axis)
    above = jnp.where(lat > 0, 1.0, 0.0).astype(F32)
    below = jnp.where(lat < lat_count - 1, 1.0, 0.0).astype(F32)
    top = pltpu.roll(wet_ref[0], 128 - rows, 1) * above
    bottom = pltpu.roll(wet_ref[2], rows, 1) * below
    wet = jnp.where(lane == 0, top, jnp.where(lane == rows + 1, bottom, wet_ref[1])).astype(BF)

    @pl.loop(0, ext, unroll=3)
    def _(r):
        outer = (r == 0) | (r == ext - 1)
        second = (r > half) & (r < ext - 1) | (r == 0)
        block = jnp.where(outer, half, lax.rem(r + half - 1, half))
        spot = pl.ds(pl.multiple_of(block * 128, 128), 128)
        high, low = halves(mixed[jnp.where(second, 1, 0), :, spot])
        both = jnp.concatenate([high, low], 1)
        spectral = lane_sum(dot(table_ref[...], jnp.concatenate([both, both], 0))) * scale
        high, low = halves(field[r])
        point = lane_sum(dot(jnp.concatenate([high, low], 1), local[...]))
        pick = lax.broadcasted_iota(jnp.int32, (128, 128), 0) == r
        cover = dot(wet, pick.astype(F32).astype(BF))
        mask[r] = cover
        value = cover * jax.nn.gelu(spectral + point + bias_ref[...], approximate=True)
        high, low = halves(value)
        both = jnp.concatenate([high, low], 1)
        for a in range(3):
            hidden[r + 2 - a, :, pl.ds(a * 256, 256)] = both

    group = 2

    @pl.loop(0, rows // group, unroll=2)
    def _(t):
        i = t * group
        block = hidden[pl.ds(i + 2, group)].reshape(group * wide, 768)
        left, middle, right = (
            lane_sum(dot(block, taps[:, pl.ds(b * 256, 256)])) for b in range(3)
        )
        total = pltpu.roll(left, 1, 0) + middle + pltpu.roll(right, group * wide - 1, 0)
        total = (total + conv_bias_ref[...]).reshape(group, wide, 128)
        total = total * mask[pl.ds(i + 1, group)]
        out[pl.ds(i, group)] = total[:, PAD : PAD + width]
        pltpu.make_async_copy(
            out.at[pl.ds(i, group)], out_hbm.at[pl.ds(i, group)], sem_out.at[t]
        ).start()

    @pl.loop(0, rows // group)
    def _(t):
        pltpu.make_async_copy(
            out.at[pl.ds(0, group)], out_hbm.at[pl.ds(0, group)], sem_out.at[t]
        ).wait()


def tail(mixed, field, wet, table, local_weight, layer_bias, conv_weight, conv_bias, rows, width, scale, lat_axis, lat_count):
    ext = rows + 2
    wide = width + 2 * PAD
    vmem = pl.BlockSpec(memory_space=pltpu.VMEM)
    hbm = pl.BlockSpec(memory_space=pl.ANY)
    return pl.pallas_call(
        functools.partial(tail_kernel, rows, width, scale, lat_axis, lat_count),
        out_shape=jax.ShapeDtypeStruct((rows, width, 128), F32),
        in_specs=[vmem] * 8,
        out_specs=hbm,
        scratch_shapes=[
            pltpu.VMEM((rows + 4, wide, 768), BF),
            pltpu.VMEM((ext, wide, 128), F32),
            pltpu.VMEM((768, 768), BF),
            pltpu.VMEM((256, 256), BF),
            pltpu.VMEM((rows, width, 128), F32),
            pltpu.SemaphoreType.DMA((rows // 2,)),
        ],
        compiler_params=pltpu.CompilerParams(vmem_limit_bytes=40 << 20),
        name="tail",
    )(mixed, field, wet, table, local_weight, layer_bias.reshape(1, 128), conv_weight, conv_bias.reshape(1, 128))


def exchange_kernel(
    zs, xs, lats, scale,
    field_hbm, ocean_hbm, modes_hbm, weight_hbm,
    mixed_out, edged, wets, table_out,
    ocean, modes, wet, table, turned, field, weight, sent, got, sums, half_a, half_b, full_a, full_b, part, up, down, halo, whole,
    load_sem, pair_sem, x_sem, z_sem, halo_sem, gz_sem, gx_sem, gp_sem, edge_sem, local_sem,
):
    rows, width, _ = field.shape
    half = rows // 2
    lanes = half * 128
    cut = lanes // 2
    wide = width + 2 * PAD
    total_lon = zs * xs * 2 * width
    lat, z, x, core = (lax.axis_index(name) for name in ("lat", "z", "x", "core"))
    other = 1 - core

    def wrap(value, size):
        return lax.rem(value + size, size)

    def device(lat=lat, z=z, x=x, core=core):
        return {"lat": lat, "z": z, "x": x, "core": core}

    def lon_at(step):
        spot = wrap((z * xs + x) * 2 + core + step, zs * xs * 2)
        return {"z": lax.div(spot, 2 * xs), "x": lax.rem(lax.div(spot, 2), xs), "core": lax.rem(spot, 2)}

    right, left, across = wrap(x + 1, xs), wrap(x - 1, xs), wrap(x + 2, xs)
    higher, lower = wrap(z + 1, zs), wrap(z - 1, zs)
    south, north = wrap(lat + 1, lats), wrap(lat - 1, lats)
    east, west = lon_at(1), lon_at(-1)

    small = [
        pltpu.make_async_copy(modes_hbm, modes, local_sem.at[12]),
        pltpu.make_async_copy(ocean_hbm, ocean, local_sem.at[13]),
    ]
    for copy in small:
        copy.start()
    for i in range(rows):
        row = (other if i < half else core) * half + i % half
        pltpu.make_async_copy(field_hbm.at[row], field.at[row], load_sem.at[row]).start()
    own_weight = pltpu.make_async_copy(weight_hbm, weight.at[core], local_sem.at[0])
    own_weight.start()

    barrier = pltpu.get_barrier_semaphore()
    beyond, behind = wrap(z + 2, zs), wrap(z - 2, zs)
    friends = [
        device(core=other), device(x=right), device(x=left), device(z=higher), device(z=lower),
        device(z=beyond), device(z=behind), device(lat=south), device(lat=north),
        device(**east), device(**west),
    ]
    for friend in friends:
        pl.semaphore_signal(barrier, inc=1, device_id=friend, device_id_type=MESH)

    for copy in small:
        copy.wait()
    count = 2 * modes.shape[1]
    slot = lax.broadcasted_iota(jnp.int32, (count // 2, count), 1)
    spread_out = lax.div(slot, 2) == lax.broadcasted_iota(jnp.int32, (count // 2, count), 0)
    pair = jnp.dot(
        jnp.broadcast_to(modes[...].astype(F32), (8, count // 2)), spread_out.astype(F32),
        precision=HIGH, preferred_element_type=F32,
    )[:1].astype(jnp.int32)
    start = ((z * xs + x) * 2 + core) * width - PAD + total_lon
    lon = start + lax.broadcasted_iota(jnp.int32, (wide, count), 0)
    odd = lax.broadcasted_iota(jnp.int32, (wide, count), 1) & 1
    phase = (pair * (lon & (total_lon - 1)) + odd * (total_lon // 4)) & (total_lon - 1)
    wave = jnp.cos(phase.astype(F32) * (2.0 * math.pi / total_lon))
    high, low = halves(wave)
    turned[:, :count] = high
    turned[:, count:] = low
    high, low = halves(wave[PAD : PAD + width].T)
    table[:, :width] = high
    table[:, width:] = low
    dry = jnp.zeros((128 - rows, width), F32)
    wet[...] = pltpu.roll(jnp.concatenate([ocean[...].astype(F32), dry], 0).T, 1, 1)

    pending = []

    def send(source, target, sems, index, where):
        copy = pltpu.make_async_remote_copy(
            src_ref=source, dst_ref=target, send_sem=sems.at[0, index], recv_sem=sems.at[1, index],
            device_id=where, device_id_type=MESH,
        )
        copy.start()
        pending.append(copy)
        return copy

    order = (4, 3, 5, 2, 6, 1, 7, 0)
    slices = [wrap(z + step, zs) for step in order]
    each = xs * 8
    group = 4 * each

    def loaded(first):
        for row in (first, first + 1):
            pltpu.make_async_copy(field_hbm.at[0], field.at[0], load_sem.at[row]).wait()

    def coefficients(first, g):
        waves = jnp.concatenate([
            table[pl.ds(pl.multiple_of(zz * each, each), each)] for zz in slices[4 * g : 4 * g + 4]
        ], 0)
        high, low = halves(jnp.concatenate([field[first], field[first + 1]], 1))
        result = dot(waves, jnp.concatenate([high, high], 0)) + dot(waves[:, :width], low)
        return result * scale

    pairs = half // 2
    pair_copies = []
    for g in range(2):
        for p in range(pairs):
            if g == 0:
                loaded(other * half + 2 * p)
            sent[g, p] = coefficients(other * half + 2 * p, g)
            if g == 0 and p == 0:
                pl.semaphore_wait(barrier, len(friends))
            pair_copies.append(
                send(sent.at[g, p], got.at[g, p], pair_sem, len(pair_copies), device(core=other))
            )
    weight_copy = send(weight_hbm, weight.at[core], halo_sem, 1, device(core=other))

    edges = []

    def edge(source, target, where):
        edges.append(send(source, target, edge_sem, len(edges), where))

    edge(field_hbm.at[rows - 1], edged.at[0, pl.ds(PAD, width)], device(lat=south))
    edge(field_hbm.at[0], edged.at[rows + 1, pl.ds(PAD, width)], device(lat=north))
    edge(wet, wets.at[0, pl.ds(PAD, width)], device(lat=south))
    edge(wet, wets.at[2, pl.ds(PAD, width)], device(lat=north))

    low_lanes, high_lanes = pl.ds(0, cut), pl.ds(cut, cut)
    firsts = []
    for g in range(2):
        for p in range(pairs):
            if g == 0:
                loaded(core * half + 2 * p)
            mine = coefficients(core * half + 2 * p, g)
            pair_copies[g * pairs + p].wait_recv()
            mine = mine + got[g, p]
            sums[pl.ds(4 * g, 4), :, :, pl.ds(p * 256, 256)] = mine.reshape(4, xs, 8, 256)
        for n in range(4 * g, 4 * g + 4):
            firsts.append((
                send(sums.at[n, across, :, low_lanes], half_a.at[n], x_sem, n, device(x=right)),
                send(sums.at[n, across, :, high_lanes], half_b.at[n], x_sem, 8 + n, device(x=left)),
            ))
    middle = pl.ds(PAD, width)
    inner = [
        pltpu.make_async_copy(field, edged.at[pl.ds(1, rows), middle], local_sem.at[1]),
        pltpu.make_async_copy(wet, wets.at[1, middle], local_sem.at[2]),
    ]
    kept_table = pltpu.make_async_copy(turned, table_out, local_sem.at[11])
    for copy in inner + [kept_table]:
        copy.start()

    seconds = []
    for n in range(len(slices)):
        firsts[n][0].wait_recv()
        sums[n, right, :, low_lanes] = sums[n, right, :, low_lanes] + half_a[n]
        to_right = send(sums.at[n, right], full_a.at[n], x_sem, 16 + n, device(x=right))
        firsts[n][1].wait_recv()
        sums[n, left, :, high_lanes] = sums[n, left, :, high_lanes] + half_b[n]
        to_left = send(sums.at[n, left], full_b.at[n], x_sem, 24 + n, device(x=left))
        seconds.append((to_right, to_left))

    def send_edges():
        for copy in edges:
            copy.wait_recv()
        for copy in inner:
            copy.wait()
        for source, target, lon in ((PAD, PAD + width, west), (width, 0, east)):
            edge(edged.at[:, pl.ds(source, PAD)], edged.at[:, pl.ds(target, PAD)], device(**lon))
            edge(wets.at[:, pl.ds(source, PAD)], wets.at[:, pl.ds(target, PAD)], device(**lon))

    rising, falling = [], []
    for n in range(len(slices)):
        seconds[n][0].wait_recv()
        seconds[n][1].wait_recv()
        total = sums[n, x] + full_a[n] + full_b[n]
        if n == 0:
            part[n] = total
            rising.append(send(part.at[n, :, low_lanes], up.at[0, :, low_lanes], z_sem, 0, device(z=beyond)))
            falling.append(send(part.at[n, :, high_lanes], down.at[0, :, high_lanes], z_sem, 4, device(z=behind)))
            send_edges()
        elif n == 7:
            for buffer, chain in ((up, rising), (down, falling)):
                for hop in (2, 3):
                    chain[hop].wait_recv()
                    total = total + buffer[hop]
        else:
            rises = n % 2 == 1
            hop = (n + 1) // 2
            chain, buffer, span = (rising, up, low_lanes) if rises else (falling, down, high_lanes)
            near, far = (higher, beyond) if rises else (lower, behind)
            part[n] = total
            if hop == 2:
                chain[0].wait_recv()
                chain[1].wait_recv()
                part[n] = part[n] + buffer[1]
                part[n, :, span] = part[n, :, span] + buffer[0, :, span]
            chain.append(send(
                part.at[n], buffer.at[hop], z_sem, (0 if rises else 4) + hop,
                device(z=far if hop == 2 else near),
            ))

    own_weight.wait()
    weight_copy.wait_recv()
    terms = jnp.concatenate([total[:, i * 128 : (i + 1) * 128] for i in range(half)], 0)
    spot = lax.rem(lax.broadcasted_iota(jnp.int32, (half * 8, 128), 0), 8)
    real, imag = jnp.zeros((half * 8, 128), F32), jnp.zeros((half * 8, 128), F32)
    for m in range(4):
        chosen = (spot == 2 * m) | (spot == 2 * m + 1)
        picked = jnp.where(chosen, terms, 0.0)
        real = real + jnp.dot(picked, weight[m // 2, m % 2, 0], precision=HIGH, preferred_element_type=F32)
        imag = imag + jnp.dot(picked, weight[m // 2, m % 2, 1], precision=HIGH, preferred_element_type=F32)
    even = lax.rem(spot, 2) == 0
    mixed = real + jnp.where(even, -pltpu.roll(imag, half * 8 - 1, 0), pltpu.roll(imag, 1, 0))
    for i in range(half):
        whole[z, x, :, pl.ds(i * 128, 128)] = mixed[i * 8 : (i + 1) * 8]
    halo[...] = jnp.where(core == 0, mixed[:8], mixed[(half - 1) * 8 :])
    tail_lanes = pl.ds(lanes, 128)
    row_copy = send(halo, whole.at[z, x, :, tail_lanes], halo_sem, 0, device(lat=wrap(lat - 1 + 2 * core, lats)))
    row_copy.wait_recv()

    front, back = pl.ds(0, cut), pl.ds(cut, lanes + 128 - cut)
    order = (0, 7, 1, 6, 2, 5, 3, 4)
    slices = [wrap(z + step, zs) for step in order]
    sideways, relays, locals_, gathered = [], [], [], []

    def spread(n):
        zz = slices[n]
        mine = whole.at[zz, x]
        sideways.append((
            send(mine, mine, gx_sem, n, device(x=right)),
            send(mine, mine, gx_sem, 8 + n, device(x=left)),
        ))

    def relay(n):
        zz = slices[n]
        sideways[n][0].wait_recv()
        from_left = whole.at[zz, left, :, front]
        first = send(from_left, from_left, gx_sem, 16 + n, device(x=right))
        sideways[n][1].wait_recv()
        from_right = whole.at[zz, right, :, back]
        second = send(from_right, from_right, gx_sem, 24 + n, device(x=left))
        relays.append((first, second))

    def finish(n):
        zz = slices[n]
        relays[n][0].wait_recv()
        relays[n][1].wait_recv()
        gathered.append(send(whole.at[zz], mixed_out.at[core, zz], gp_sem, n, device(core=other)))
        kept = pltpu.make_async_copy(whole.at[zz], mixed_out.at[core, zz], local_sem.at[3 + n])
        kept.start()
        locals_.append(kept)

    def along(n, where, index, span=None):
        source = whole.at[slices[n], x] if span is None else whole.at[slices[n], x, :, span]
        return send(source, source, gz_sem, index, device(z=where))

    far_up, far_down = along(0, beyond, 2), along(0, behind, 3)
    near_up, near_down = along(0, higher, 0), along(0, lower, 1)
    spread(0)
    near_up.wait_recv()
    spread(1)
    near_down.wait_recv()
    spread(2)
    far_up.wait_recv()
    next_up, half_up = along(3, higher, 4), along(3, beyond, 6, front)
    far_down.wait_recv()
    next_down, half_down = along(4, lower, 5), along(4, behind, 7, back)
    spread(3)
    spread(4)
    for n in range(3):
        relay(n)
    next_up.wait_recv()
    spread(5)
    next_down.wait_recv()
    spread(6)
    half_up.wait_recv()
    half_down.wait_recv()
    spread(7)
    finish(0)
    for n in range(3, 8):
        relay(n)
        finish(n - 2)
    finish(6)
    finish(7)

    for copy in edges[4:] + gathered:
        copy.wait_recv()
    for copy in pending:
        copy.wait_send()
    for copy in locals_ + [kept_table]:
        copy.wait()


def exchange(field, ocean, modes, weight, lats, zs, xs, scale):
    rows, width, _ = field.shape
    wide = width + 2 * PAD
    lanes = rows // 2 * 128
    hbm = pl.BlockSpec(memory_space=pl.ANY)
    dma = pltpu.SemaphoreType.DMA
    return pl.pallas_call(
        functools.partial(exchange_kernel, zs, xs, lats, scale),
        out_shape=(
            jax.ShapeDtypeStruct((2, zs, xs, 8, lanes + 128), F32),
            jax.ShapeDtypeStruct((rows + 2, wide, 128), F32),
            jax.ShapeDtypeStruct((3, wide, 128), F32),
            jax.ShapeDtypeStruct((wide, 512), BF),
        ),
        in_specs=[hbm] * 4,
        out_specs=(hbm, hbm, hbm, hbm),
        scratch_shapes=[
            pltpu.VMEM(ocean.shape, jnp.int32),
            pltpu.VMEM((1, modes.size), jnp.int32),
            pltpu.VMEM((width, 128), F32),
            pltpu.VMEM((256, 2 * width), BF),
            pltpu.VMEM((wide, 512), BF),
            pltpu.VMEM((rows, width, 128), F32),
            pltpu.VMEM((2, *weight.shape), F32),
            pltpu.VMEM((2, rows // 4, 128, 256), F32),
            pltpu.VMEM((2, rows // 4, 128, 256), F32),
            pltpu.VMEM((zs, xs, 8, lanes), F32),
            pltpu.VMEM((zs, 8, lanes // 2), F32),
            pltpu.VMEM((zs, 8, lanes // 2), F32),
            pltpu.VMEM((zs, 8, lanes), F32),
            pltpu.VMEM((zs, 8, lanes), F32),
            pltpu.VMEM((zs, 8, lanes), F32),
            pltpu.VMEM((4, 8, lanes), F32),
            pltpu.VMEM((4, 8, lanes), F32),
            pltpu.VMEM((8, 128), F32),
            pltpu.VMEM((zs, xs, 8, lanes + 128), F32),
            dma((rows,)), dma((2, 8)), dma((2, 32)), dma((2, 8)), dma((2, 2)), dma((2, 8)),
            dma((2, 32)), dma((2, 8)), dma((2, 8)), dma((14,)),
        ],
        compiler_params=pltpu.CompilerParams(
            collective_id=0, has_side_effects=True, vmem_limit_bytes=32 << 20
        ),
        name="exchange",
    )(*(pltpu.with_memory_space_constraint(a, pltpu.HBM) for a in (field, ocean, modes.reshape(1, -1), weight)))


def per_device(field, ocean, modes, spectral_weight, local_weight, layer_bias, conv_weight, conv_bias):
    rows, width, channels = field.shape
    lats, zs, xs = (lax.axis_size(name) for name in ("lat", "z", "x"))
    total_lon = width * zs * xs * 2
    total_modes = modes.shape[0]
    mixed, edged, wets, inverse = exchange(
        field, ocean, modes, spectral_weight, lats, zs, xs, 1.0 / math.sqrt(total_lon)
    )
    mixed = mixed.reshape(2, 2 * total_modes, -1)
    return tail(
        mixed, edged, wets, inverse, local_weight, layer_bias,
        conv_weight, conv_bias, rows, width, 2.0 / math.sqrt(total_modes), "lat", lats,
    )


def solution(mesh):
    split = Mesh(mesh.devices.reshape(mesh.shape["lat"], 8, 4, 2), ("lat", *LON))
    placed = (P("lat", LON, None), P("lat", LON), P(), P(LON, None, None, None), P(), P(), P(), P())
    return jax.shard_map(
        per_device, mesh=split, in_specs=placed, out_specs=P("lat", LON, None), check_vma=False
    )
```

```python
import functools
import math

import jax
import jax.numpy as jnp
from jax import lax
from jax.experimental import pallas as pl
from jax.experimental.pallas import tpu as pltpu
from jax.sharding import Mesh
from jax.sharding import PartitionSpec as P

LON = ("z", "x", "core")
HIGH = lax.Precision.HIGHEST
MESH = pl.DeviceIdType.MESH
PAD = 8
BF = jnp.bfloat16
F32 = jnp.float32


def halves(value):
    high = value.astype(BF)
    return high, (value - high.astype(F32)).astype(BF)


def dot(a, b):
    return jnp.dot(a, b, preferred_element_type=F32)


def lane_sum(acc):
    return acc[:, :128] + acc[:, 128:]


def tail_kernel(
    rows, width, scale, lat_axis, lat_count,
    mixed, field, wet_ref, table_ref, local_ref, bias_ref, conv_ref, conv_bias_ref,
    out_hbm,
    hidden, mask, taps, local, out, sem_out,
):
    ext = rows + 2
    wide = width + 2 * PAD
    half = rows // 2

    high, low = halves(local_ref[...])
    both = jnp.concatenate([high, low], 1)
    local[0:128] = both
    local[128:256] = both
    for a in range(3):
        for b in range(3):
            high, low = halves(conv_ref[a, b])
            both = jnp.concatenate([high, low], 1)
            for q in range(2):
                taps[pl.ds(a * 256 + q * 128, 128), pl.ds(b * 256, 256)] = both

    lane = lax.broadcasted_iota(jnp.int32, (wide, 128), 1)
    lat = lax.axis_index(lat_axis)
    above = jnp.where(lat > 0, 1.0, 0.0).astype(F32)
    below = jnp.where(lat < lat_count - 1, 1.0, 0.0).astype(F32)
    top = pltpu.roll(wet_ref[0], 128 - rows, 1) * above
    bottom = pltpu.roll(wet_ref[2], rows, 1) * below
    wet = jnp.where(lane == 0, top, jnp.where(lane == rows + 1, bottom, wet_ref[1])).astype(BF)

    @pl.loop(0, ext, unroll=6)
    def _(r):
        outer = (r == 0) | (r == ext - 1)
        second = (r > half) & (r < ext - 1) | (r == 0)
        block = jnp.where(outer, half, lax.rem(r + half - 1, half))
        spot = pl.ds(pl.multiple_of(block * 128, 128), 128)
        high, low = halves(mixed[jnp.where(second, 1, 0), :, spot])
        both = jnp.concatenate([high, low], 1)
        spectral = lane_sum(dot(table_ref[...], jnp.concatenate([both, both], 0))) * scale
        high, low = halves(field[r])
        point = lane_sum(dot(jnp.concatenate([high, low], 1), local[...]))
        pick = lax.broadcasted_iota(jnp.int32, (128, 128), 0) == r
        cover = dot(wet, pick.astype(F32).astype(BF))
        mask[r] = cover
        value = cover * jax.nn.gelu(spectral + point + bias_ref[...], approximate=True)
        high, low = halves(value)
        both = jnp.concatenate([high, low], 1)
        for a in range(3):
            hidden[r + 2 - a, :, pl.ds(a * 256, 256)] = both

    group = 4

    @pl.loop(0, rows // group, unroll=4)
    def _(t):
        i = t * group
        block = hidden[pl.ds(i + 2, group)].reshape(group * wide, 768)
        left, middle, right = (
            lane_sum(dot(block, taps[:, pl.ds(b * 256, 256)])) for b in range(3)
        )
        total = pltpu.roll(left, 1, 0) + middle + pltpu.roll(right, group * wide - 1, 0)
        total = (total + conv_bias_ref[...]).reshape(group, wide, 128)
        total = total * mask[pl.ds(i + 1, group)]
        out[pl.ds(i, group)] = total[:, PAD : PAD + width]
        pltpu.make_async_copy(
            out.at[pl.ds(i, group)], out_hbm.at[pl.ds(i, group)], sem_out.at[t]
        ).start()

    @pl.loop(0, rows // group)
    def _(t):
        pltpu.make_async_copy(
            out.at[pl.ds(0, group)], out_hbm.at[pl.ds(0, group)], sem_out.at[t]
        ).wait()


def tail(mixed, field, wet, table, local_weight, layer_bias, conv_weight, conv_bias, rows, width, scale, lat_axis, lat_count):
    ext = rows + 2
    wide = width + 2 * PAD
    vmem = pl.BlockSpec(memory_space=pltpu.VMEM)
    hbm = pl.BlockSpec(memory_space=pl.ANY)
    return pl.pallas_call(
        functools.partial(tail_kernel, rows, width, scale, lat_axis, lat_count),
        out_shape=jax.ShapeDtypeStruct((rows, width, 128), F32),
        in_specs=[vmem] * 8,
        out_specs=hbm,
        scratch_shapes=[
            pltpu.VMEM((rows + 4, wide, 768), BF),
            pltpu.VMEM((ext, wide, 128), F32),
            pltpu.VMEM((768, 768), BF),
            pltpu.VMEM((256, 256), BF),
            pltpu.VMEM((rows, width, 128), F32),
            pltpu.SemaphoreType.DMA((rows // 2,)),
        ],
        compiler_params=pltpu.CompilerParams(vmem_limit_bytes=40 << 20),
        name="tail",
    )(mixed, field, wet, table, local_weight, layer_bias.reshape(1, 128), conv_weight, conv_bias.reshape(1, 128))


def exchange_kernel(
    zs, xs, lats, scale,
    field_hbm, ocean_hbm, modes_hbm, weight_hbm,
    mixed_out, edged, wets, table_out,
    ocean, modes, wet, table, turned, field, weight, sent, got, sums, half_a, half_b, full_a, full_b, part, up, down, halo, whole,
    load_sem, pair_sem, x_sem, z_sem, halo_sem, gz_sem, gx_sem, gp_sem, edge_sem, local_sem,
):
    rows, width, _ = field.shape
    half = rows // 2
    lanes = half * 128
    cut = lanes // 2
    wide = width + 2 * PAD
    total_lon = zs * xs * 2 * width
    lat, z, x, core = (lax.axis_index(name) for name in ("lat", "z", "x", "core"))
    other = 1 - core

    def wrap(value, size):
        return lax.rem(value + size, size)

    def device(lat=lat, z=z, x=x, core=core):
        return {"lat": lat, "z": z, "x": x, "core": core}

    def lon_at(step):
        spot = wrap((z * xs + x) * 2 + core + step, zs * xs * 2)
        return {"z": lax.div(spot, 2 * xs), "x": lax.rem(lax.div(spot, 2), xs), "core": lax.rem(spot, 2)}

    right, left, across = wrap(x + 1, xs), wrap(x - 1, xs), wrap(x + 2, xs)
    higher, lower = wrap(z + 1, zs), wrap(z - 1, zs)
    south, north = wrap(lat + 1, lats), wrap(lat - 1, lats)
    east, west = lon_at(1), lon_at(-1)

    small = [
        pltpu.make_async_copy(modes_hbm, modes, local_sem.at[12]),
        pltpu.make_async_copy(ocean_hbm, ocean, local_sem.at[13]),
    ]
    for copy in small:
        copy.start()
    for i in range(rows):
        row = (other if i < half else core) * half + i % half
        pltpu.make_async_copy(field_hbm.at[row], field.at[row], load_sem.at[row]).start()
    own_weight = pltpu.make_async_copy(weight_hbm, weight.at[core], local_sem.at[0])
    own_weight.start()

    barrier = pltpu.get_barrier_semaphore()
    beyond, behind = wrap(z + 2, zs), wrap(z - 2, zs)
    friends = [
        device(core=other), device(x=right), device(x=left), device(z=higher), device(z=lower),
        device(z=beyond), device(z=behind), device(lat=south), device(lat=north),
        device(**east), device(**west),
    ]
    for friend in friends:
        pl.semaphore_signal(barrier, inc=1, device_id=friend, device_id_type=MESH)

    for copy in small:
        copy.wait()
    count = 2 * modes.shape[1]
    slot = lax.broadcasted_iota(jnp.int32, (count // 2, count), 1)
    spread_out = lax.div(slot, 2) == lax.broadcasted_iota(jnp.int32, (count // 2, count), 0)
    pair = jnp.dot(
        jnp.broadcast_to(modes[...].astype(F32), (8, count // 2)), spread_out.astype(F32),
        precision=HIGH, preferred_element_type=F32,
    )[:1].astype(jnp.int32)
    start = ((z * xs + x) * 2 + core) * width - PAD + total_lon
    lon = start + lax.broadcasted_iota(jnp.int32, (wide, count), 0)
    odd = lax.broadcasted_iota(jnp.int32, (wide, count), 1) & 1
    phase = (pair * (lon & (total_lon - 1)) + odd * (total_lon // 4)) & (total_lon - 1)
    wave = jnp.cos(phase.astype(F32) * (2.0 * math.pi / total_lon))
    high, low = halves(wave)
    turned[:, :count] = high
    turned[:, count:] = low
    high, low = halves(wave[PAD : PAD + width].T)
    table[:, :width] = high
    table[:, width:] = low
    dry = jnp.zeros((128 - rows, width), F32)
    wet[...] = pltpu.roll(jnp.concatenate([ocean[...].astype(F32), dry], 0).T, 1, 1)

    pending = []

    def send(source, target, sems, index, where):
        copy = pltpu.make_async_remote_copy(
            src_ref=source, dst_ref=target, send_sem=sems.at[0, index], recv_sem=sems.at[1, index],
            device_id=where, device_id_type=MESH,
        )
        copy.start()
        pending.append(copy)
        return copy

    order = (4, 3, 5, 2, 6, 1, 7, 0)
    slices = [wrap(z + step, zs) for step in order]
    each = xs * 8
    group = 4 * each

    def loaded(first):
        for row in (first, first + 1):
            pltpu.make_async_copy(field_hbm.at[0], field.at[0], load_sem.at[row]).wait()

    def coefficients(first, g):
        waves = jnp.concatenate([
            table[pl.ds(pl.multiple_of(zz * each, each), each)] for zz in slices[4 * g : 4 * g + 4]
        ], 0)
        high, low = halves(jnp.concatenate([field[first], field[first + 1]], 1))
        result = dot(waves, jnp.concatenate([high, high], 0)) + dot(waves[:, :width], low)
        return result * scale

    pairs = half // 2
    pair_copies = []
    for g in range(2):
        for p in range(pairs):
            if g == 0:
                loaded(other * half + 2 * p)
            sent[g, p] = coefficients(other * half + 2 * p, g)
            if g == 0 and p == 0:
                pl.semaphore_wait(barrier, len(friends))
            pair_copies.append(
                send(sent.at[g, p], got.at[g, p], pair_sem, len(pair_copies), device(core=other))
            )
    weight_copy = send(weight_hbm, weight.at[core], halo_sem, 1, device(core=other))

    edges = []

    def edge(source, target, where):
        edges.append(send(source, target, edge_sem, len(edges), where))

    edge(field_hbm.at[rows - 1], edged.at[0, pl.ds(PAD, width)], device(lat=south))
    edge(field_hbm.at[0], edged.at[rows + 1, pl.ds(PAD, width)], device(lat=north))
    edge(wet, wets.at[0, pl.ds(PAD, width)], device(lat=south))
    edge(wet, wets.at[2, pl.ds(PAD, width)], device(lat=north))

    low_lanes, high_lanes = pl.ds(0, cut), pl.ds(cut, cut)
    firsts = []
    for g in range(2):
        for p in range(pairs):
            if g == 0:
                loaded(core * half + 2 * p)
            mine = coefficients(core * half + 2 * p, g)
            pair_copies[g * pairs + p].wait_recv()
            mine = mine + got[g, p]
            sums[pl.ds(4 * g, 4), :, :, pl.ds(p * 256, 256)] = mine.reshape(4, xs, 8, 256)
        for n in range(4 * g, 4 * g + 4):
            firsts.append((
                send(sums.at[n, across, :, low_lanes], half_a.at[n], x_sem, n, device(x=right)),
                send(sums.at[n, across, :, high_lanes], half_b.at[n], x_sem, 8 + n, device(x=left)),
            ))
    middle = pl.ds(PAD, width)
    inner = [
        pltpu.make_async_copy(field, edged.at[pl.ds(1, rows), middle], local_sem.at[1]),
        pltpu.make_async_copy(wet, wets.at[1, middle], local_sem.at[2]),
    ]
    kept_table = pltpu.make_async_copy(turned, table_out, local_sem.at[11])
    for copy in inner + [kept_table]:
        copy.start()

    seconds = []
    for n in range(len(slices)):
        firsts[n][0].wait_recv()
        sums[n, right, :, low_lanes] = sums[n, right, :, low_lanes] + half_a[n]
        to_right = send(sums.at[n, right], full_a.at[n], x_sem, 16 + n, device(x=right))
        firsts[n][1].wait_recv()
        sums[n, left, :, high_lanes] = sums[n, left, :, high_lanes] + half_b[n]
        to_left = send(sums.at[n, left], full_b.at[n], x_sem, 24 + n, device(x=left))
        seconds.append((to_right, to_left))

    def send_edges():
        for copy in edges:
            copy.wait_recv()
        for copy in inner:
            copy.wait()
        for source, target, lon in ((PAD, PAD + width, west), (width, 0, east)):
            edge(edged.at[:, pl.ds(source, PAD)], edged.at[:, pl.ds(target, PAD)], device(**lon))
            edge(wets.at[:, pl.ds(source, PAD)], wets.at[:, pl.ds(target, PAD)], device(**lon))

    rising, falling = [], []
    for n in range(len(slices)):
        seconds[n][0].wait_recv()
        seconds[n][1].wait_recv()
        total = sums[n, x] + full_a[n] + full_b[n]
        if n == 0:
            part[n] = total
            rising.append(send(part.at[n, :, low_lanes], up.at[0, :, low_lanes], z_sem, 0, device(z=beyond)))
            falling.append(send(part.at[n, :, high_lanes], down.at[0, :, high_lanes], z_sem, 4, device(z=behind)))
            send_edges()
        elif n == 7:
            for buffer, chain in ((up, rising), (down, falling)):
                for hop in (2, 3):
                    chain[hop].wait_recv()
                    total = total + buffer[hop]
        else:
            rises = n % 2 == 1
            hop = (n + 1) // 2
            chain, buffer, span = (rising, up, low_lanes) if rises else (falling, down, high_lanes)
            near, far = (higher, beyond) if rises else (lower, behind)
            part[n] = total
            if hop == 2:
                chain[0].wait_recv()
                chain[1].wait_recv()
                part[n] = part[n] + buffer[1]
                part[n, :, span] = part[n, :, span] + buffer[0, :, span]
            chain.append(send(
                part.at[n], buffer.at[hop], z_sem, (0 if rises else 4) + hop,
                device(z=far if hop == 2 else near),
            ))

    own_weight.wait()
    weight_copy.wait_recv()
    terms = jnp.concatenate([total[:, i * 128 : (i + 1) * 128] for i in range(half)], 0)
    spot = lax.rem(lax.broadcasted_iota(jnp.int32, (half * 8, 128), 0), 8)
    real, imag = jnp.zeros((half * 8, 128), F32), jnp.zeros((half * 8, 128), F32)
    for m in range(4):
        chosen = (spot == 2 * m) | (spot == 2 * m + 1)
        picked = jnp.where(chosen, terms, 0.0)
        real = real + jnp.dot(picked, weight[m // 2, m % 2, 0], precision=HIGH, preferred_element_type=F32)
        imag = imag + jnp.dot(picked, weight[m // 2, m % 2, 1], precision=HIGH, preferred_element_type=F32)
    even = lax.rem(spot, 2) == 0
    mixed = real + jnp.where(even, -pltpu.roll(imag, half * 8 - 1, 0), pltpu.roll(imag, 1, 0))
    for i in range(half):
        whole[:, pl.ds(i * 128, 128)] = mixed[i * 8 : (i + 1) * 8]
    halo[...] = jnp.where(core == 0, mixed[:8], mixed[(half - 1) * 8 :])
    tail_lanes = pl.ds(lanes, 128)
    row_copy = send(halo, whole.at[:, tail_lanes], halo_sem, 0, device(lat=wrap(lat - 1 + 2 * core, lats)))
    row_copy.wait_recv()
    kept = pltpu.make_async_copy(whole, mixed_out.at[core, z, x], local_sem.at[3])
    kept.start()

    front, back = pl.ds(0, cut), pl.ds(cut, lanes + 128 - cut)
    order = (0, 7, 1, 6, 2, 5, 3, 4)
    slices = [wrap(z + step, zs) for step in order]
    sideways, relays, gathered = [], [], []

    def spread(n):
        zz = slices[n]
        mine = mixed_out.at[core, zz, x]
        source = whole if n == 0 else mine
        sideways.append((
            send(source, mine, gx_sem, n, device(x=right)),
            send(source, mine, gx_sem, 8 + n, device(x=left)),
        ))

    def relay(n):
        zz = slices[n]
        sideways[n][0].wait_recv()
        from_left = mixed_out.at[core, zz, left, :, front]
        first = send(from_left, from_left, gx_sem, 16 + n, device(x=right))
        sideways[n][1].wait_recv()
        from_right = mixed_out.at[core, zz, right, :, back]
        second = send(from_right, from_right, gx_sem, 24 + n, device(x=left))
        relays.append((first, second))

    def finish(n):
        zz = slices[n]
        relays[n][0].wait_recv()
        relays[n][1].wait_recv()
        if n == 0:
            kept.wait()
        done = mixed_out.at[core, zz]
        gathered.append(send(done, done, gp_sem, n, device(core=other)))

    def along(n, where, index, span=None):
        spot = mixed_out.at[core, slices[n], x]
        if span is not None:
            spot = mixed_out.at[core, slices[n], x, :, span]
        return send(whole if n == 0 else spot, spot, gz_sem, index, device(z=where))

    far_up, far_down = along(0, beyond, 2), along(0, behind, 3)
    near_up, near_down = along(0, higher, 0), along(0, lower, 1)
    spread(0)
    near_up.wait_recv()
    spread(1)
    near_down.wait_recv()
    spread(2)
    far_up.wait_recv()
    next_up = along(3, higher, 4)
    half_up = along(3, beyond, 6, front)
    far_down.wait_recv()
    next_down = along(4, lower, 5)
    half_down = along(4, behind, 7, back)
    spread(3)
    spread(4)
    for n in range(3):
        relay(n)
    next_up.wait_recv()
    spread(5)
    next_down.wait_recv()
    spread(6)
    relay(3)
    relay(4)
    finish(0)
    half_up.wait_recv()
    half_down.wait_recv()
    spread(7)
    relay(5)
    finish(1)
    finish(2)
    relay(6)
    finish(3)
    finish(4)
    relay(7)
    for n in range(5, 8):
        finish(n)

    for copy in edges[4:] + gathered:
        copy.wait_recv()
    for copy in pending:
        copy.wait_send()
    kept_table.wait()


def exchange(field, ocean, modes, weight, lats, zs, xs, scale):
    rows, width, _ = field.shape
    wide = width + 2 * PAD
    lanes = rows // 2 * 128
    hbm = pl.BlockSpec(memory_space=pl.ANY)
    dma = pltpu.SemaphoreType.DMA
    return pl.pallas_call(
        functools.partial(exchange_kernel, zs, xs, lats, scale),
        out_shape=(
            jax.ShapeDtypeStruct((2, zs, xs, 8, lanes + 128), F32),
            jax.ShapeDtypeStruct((rows + 2, wide, 128), F32),
            jax.ShapeDtypeStruct((3, wide, 128), F32),
            jax.ShapeDtypeStruct((wide, 512), BF),
        ),
        in_specs=[hbm] * 4,
        out_specs=(hbm, hbm, hbm, hbm),
        scratch_shapes=[
            pltpu.VMEM(ocean.shape, jnp.int32),
            pltpu.VMEM((1, modes.size), jnp.int32),
            pltpu.VMEM((width, 128), F32),
            pltpu.VMEM((256, 2 * width), BF),
            pltpu.VMEM((wide, 512), BF),
            pltpu.VMEM((rows, width, 128), F32),
            pltpu.VMEM((2, *weight.shape), F32),
            pltpu.VMEM((2, rows // 4, 128, 256), F32),
            pltpu.VMEM((2, rows // 4, 128, 256), F32),
            pltpu.VMEM((zs, xs, 8, lanes), F32),
            pltpu.VMEM((zs, 8, lanes // 2), F32),
            pltpu.VMEM((zs, 8, lanes // 2), F32),
            pltpu.VMEM((zs, 8, lanes), F32),
            pltpu.VMEM((zs, 8, lanes), F32),
            pltpu.VMEM((zs, 8, lanes), F32),
            pltpu.VMEM((4, 8, lanes), F32),
            pltpu.VMEM((4, 8, lanes), F32),
            pltpu.VMEM((8, 128), F32),
            pltpu.VMEM((8, lanes + 128), F32),
            dma((rows,)), dma((2, 8)), dma((2, 32)), dma((2, 8)), dma((2, 2)), dma((2, 8)),
            dma((2, 32)), dma((2, 8)), dma((2, 8)), dma((14,)),
        ],
        compiler_params=pltpu.CompilerParams(
            collective_id=0, has_side_effects=True, vmem_limit_bytes=32 << 20
        ),
        name="exchange",
    )(*(pltpu.with_memory_space_constraint(a, pltpu.HBM) for a in (field, ocean, modes.reshape(1, -1), weight)))


def per_device(field, ocean, modes, spectral_weight, local_weight, layer_bias, conv_weight, conv_bias):
    rows, width, channels = field.shape
    lats, zs, xs = (lax.axis_size(name) for name in ("lat", "z", "x"))
    total_lon = width * zs * xs * 2
    total_modes = modes.shape[0]
    mixed, edged, wets, inverse = exchange(
        field, ocean, modes, spectral_weight, lats, zs, xs, 1.0 / math.sqrt(total_lon)
    )
    mixed = mixed.reshape(2, 2 * total_modes, -1)
    return tail(
        mixed, edged, wets, inverse, local_weight, layer_bias,
        conv_weight, conv_bias, rows, width, 2.0 / math.sqrt(total_modes), "lat", lats,
    )


def solution(mesh):
    split = Mesh(mesh.devices.reshape(mesh.shape["lat"], 8, 4, 2), ("lat", *LON))
    placed = (P("lat", LON, None), P("lat", LON), P(), P(LON, None, None, None), P(), P(), P(), P())
    return jax.shard_map(
        per_device, mesh=split, in_specs=placed, out_specs=P("lat", LON, None), check_vma=False
    )
```

```python
import functools
import math

import jax
import jax.numpy as jnp
from jax import lax
from jax.experimental import pallas as pl
from jax.experimental.pallas import tpu as pltpu
from jax.sharding import Mesh
from jax.sharding import PartitionSpec as P

LON = ("z", "x", "core")
HIGH = lax.Precision.HIGHEST
MESH = pl.DeviceIdType.MESH
PAD = 8
BF = jnp.bfloat16
F32 = jnp.float32


def halves(value):
    high = value.astype(BF)
    return high, (value - high.astype(F32)).astype(BF)


def dot(a, b):
    return jnp.dot(a, b, preferred_element_type=F32)


def lane_sum(acc):
    return acc[:, :128] + acc[:, 128:]


def tail_kernel(
    rows, width, scale, lat_axis, lat_count,
    mixed, field, wet_ref, table_ref, local_ref, bias_ref, conv_ref, conv_bias_ref,
    out_hbm,
    hidden, mask, taps, local, out, sem_out,
):
    ext = rows + 2
    wide = width + 2 * PAD
    half = rows // 2

    high, low = halves(local_ref[...])
    both = jnp.concatenate([high, low], 1)
    local[0:128] = both
    local[128:256] = both
    for a in range(3):
        for b in range(3):
            high, low = halves(conv_ref[a, b])
            both = jnp.concatenate([high, low], 1)
            for q in range(2):
                taps[pl.ds(a * 256 + q * 128, 128), pl.ds(b * 256, 256)] = both

    lane = lax.broadcasted_iota(jnp.int32, (wide, 128), 1)
    lat = lax.axis_index(lat_axis)
    above = jnp.where(lat > 0, 1.0, 0.0).astype(F32)
    below = jnp.where(lat < lat_count - 1, 1.0, 0.0).astype(F32)
    top = pltpu.roll(wet_ref[0], 128 - rows, 1) * above
    bottom = pltpu.roll(wet_ref[2], rows, 1) * below
    wet = jnp.where(lane == 0, top, jnp.where(lane == rows + 1, bottom, wet_ref[1])).astype(BF)

    @pl.loop(0, ext, unroll=6)
    def _(r):
        outer = (r == 0) | (r == ext - 1)
        second = (r > half) & (r < ext - 1) | (r == 0)
        block = jnp.where(outer, half, lax.rem(r + half - 1, half))
        spot = pl.ds(pl.multiple_of(block * 128, 128), 128)
        high, low = halves(mixed[jnp.where(second, 1, 0), :, spot])
        both = jnp.concatenate([high, low], 1)
        spectral = lane_sum(dot(table_ref[...], jnp.concatenate([both, both], 0))) * scale
        high, low = halves(field[r])
        point = lane_sum(dot(jnp.concatenate([high, low], 1), local[...]))
        pick = lax.broadcasted_iota(jnp.int32, (128, 128), 0) == r
        cover = dot(wet, pick.astype(F32).astype(BF))
        mask[r] = cover
        value = cover * jax.nn.gelu(spectral + point + bias_ref[...], approximate=True)
        high, low = halves(value)
        both = jnp.concatenate([high, low], 1)
        for a in range(3):
            hidden[r + 2 - a, :, pl.ds(a * 256, 256)] = both

    group = 4

    @pl.loop(0, rows // group, unroll=4)
    def _(t):
        i = t * group
        block = hidden[pl.ds(i + 2, group)].reshape(group * wide, 768)
        left, middle, right = (
            lane_sum(dot(block, taps[:, pl.ds(b * 256, 256)])) for b in range(3)
        )
        total = pltpu.roll(left, 1, 0) + middle + pltpu.roll(right, group * wide - 1, 0)
        total = (total + conv_bias_ref[...]).reshape(group, wide, 128)
        total = total * mask[pl.ds(i + 1, group)]
        out[pl.ds(i, group)] = total[:, PAD : PAD + width]
        pltpu.make_async_copy(
            out.at[pl.ds(i, group)], out_hbm.at[pl.ds(i, group)], sem_out.at[t]
        ).start()

    @pl.loop(0, rows // group)
    def _(t):
        pltpu.make_async_copy(
            out.at[pl.ds(0, group)], out_hbm.at[pl.ds(0, group)], sem_out.at[t]
        ).wait()


def tail(mixed, field, wet, table, local_weight, layer_bias, conv_weight, conv_bias, rows, width, scale, lat_axis, lat_count):
    ext = rows + 2
    wide = width + 2 * PAD
    vmem = pl.BlockSpec(memory_space=pltpu.VMEM)
    hbm = pl.BlockSpec(memory_space=pl.ANY)
    return pl.pallas_call(
        functools.partial(tail_kernel, rows, width, scale, lat_axis, lat_count),
        out_shape=jax.ShapeDtypeStruct((rows, width, 128), F32),
        in_specs=[vmem] * 8,
        out_specs=hbm,
        scratch_shapes=[
            pltpu.VMEM((rows + 4, wide, 768), BF),
            pltpu.VMEM((ext, wide, 128), F32),
            pltpu.VMEM((768, 768), BF),
            pltpu.VMEM((256, 256), BF),
            pltpu.VMEM((rows, width, 128), F32),
            pltpu.SemaphoreType.DMA((rows // 2,)),
        ],
        compiler_params=pltpu.CompilerParams(vmem_limit_bytes=40 << 20),
        name="tail",
    )(mixed, field, wet, table, local_weight, layer_bias.reshape(1, 128), conv_weight, conv_bias.reshape(1, 128))


def exchange_kernel(
    zs, xs, lats, scale,
    field_hbm, ocean_hbm, modes_hbm, weight_hbm,
    mixed_out, edged, wets, table_out,
    ocean, modes, wet, table, turned, field, weight, sent, got, sums, half_a, half_b, full_a, full_b, part, up, down, halo, whole,
    load_sem, pair_sem, x_sem, z_sem, halo_sem, gz_sem, gx_sem, gp_sem, edge_sem, local_sem,
):
    rows, width, _ = field.shape
    half = rows // 2
    lanes = half * 128
    cut = lanes // 2
    wide = width + 2 * PAD
    total_lon = zs * xs * 2 * width
    lat, z, x, core = (lax.axis_index(name) for name in ("lat", "z", "x", "core"))
    other = 1 - core

    def wrap(value, size):
        return lax.rem(value + size, size)

    def device(lat=lat, z=z, x=x, core=core):
        return {"lat": lat, "z": z, "x": x, "core": core}

    def lon_at(step):
        spot = wrap((z * xs + x) * 2 + core + step, zs * xs * 2)
        return {"z": lax.div(spot, 2 * xs), "x": lax.rem(lax.div(spot, 2), xs), "core": lax.rem(spot, 2)}

    right, left, across = wrap(x + 1, xs), wrap(x - 1, xs), wrap(x + 2, xs)
    higher, lower = wrap(z + 1, zs), wrap(z - 1, zs)
    south, north = wrap(lat + 1, lats), wrap(lat - 1, lats)
    east, west = lon_at(1), lon_at(-1)

    small = [
        pltpu.make_async_copy(modes_hbm, modes, local_sem.at[12]),
        pltpu.make_async_copy(ocean_hbm, ocean, local_sem.at[13]),
    ]
    for copy in small:
        copy.start()
    for i in range(rows):
        row = (other if i < half else core) * half + i % half
        pltpu.make_async_copy(field_hbm.at[row], field.at[row], load_sem.at[row]).start()
    own_weight = pltpu.make_async_copy(weight_hbm, weight.at[core], local_sem.at[0])
    own_weight.start()

    barrier = pltpu.get_barrier_semaphore()
    beyond, behind = wrap(z + 2, zs), wrap(z - 2, zs)
    friends = [
        device(core=other), device(x=right), device(x=left), device(z=higher), device(z=lower),
        device(z=beyond), device(z=behind), device(lat=south), device(lat=north),
        device(**east), device(**west),
    ]
    for friend in friends:
        pl.semaphore_signal(barrier, inc=1, device_id=friend, device_id_type=MESH)

    for copy in small:
        copy.wait()
    count = 2 * modes.shape[1]
    slot = lax.broadcasted_iota(jnp.int32, (count // 2, count), 1)
    spread_out = lax.div(slot, 2) == lax.broadcasted_iota(jnp.int32, (count // 2, count), 0)
    pair = jnp.dot(
        jnp.broadcast_to(modes[...].astype(F32), (8, count // 2)), spread_out.astype(F32),
        precision=HIGH, preferred_element_type=F32,
    )[:1].astype(jnp.int32)
    start = ((z * xs + x) * 2 + core) * width - PAD + total_lon
    lon = start + lax.broadcasted_iota(jnp.int32, (wide, count), 0)
    odd = lax.broadcasted_iota(jnp.int32, (wide, count), 1) & 1
    phase = (pair * (lon & (total_lon - 1)) + odd * (total_lon // 4)) & (total_lon - 1)
    wave = jnp.cos(phase.astype(F32) * (2.0 * math.pi / total_lon))
    high, low = halves(wave)
    turned[:, :count] = high
    turned[:, count:] = low
    high, low = halves(wave[PAD : PAD + width].T)
    table[:, :width] = high
    table[:, width:] = low
    dry = jnp.zeros((128 - rows, width), F32)
    wet[...] = pltpu.roll(jnp.concatenate([ocean[...].astype(F32), dry], 0).T, 1, 1)

    pending = []

    def send(source, target, sems, index, where):
        copy = pltpu.make_async_remote_copy(
            src_ref=source, dst_ref=target, send_sem=sems.at[0, index], recv_sem=sems.at[1, index],
            device_id=where, device_id_type=MESH,
        )
        copy.start()
        pending.append(copy)
        return copy

    order = (4, 3, 5, 2, 6, 1, 7, 0)
    slices = [wrap(z + step, zs) for step in order]
    each = xs * 8
    group = 4 * each

    def loaded(first):
        for row in (first, first + 1):
            pltpu.make_async_copy(field_hbm.at[0], field.at[0], load_sem.at[row]).wait()

    def coefficients(first, g):
        waves = jnp.concatenate([
            table[pl.ds(pl.multiple_of(zz * each, each), each)] for zz in slices[4 * g : 4 * g + 4]
        ], 0)
        high, low = halves(jnp.concatenate([field[first], field[first + 1]], 1))
        result = dot(waves, jnp.concatenate([high, high], 0)) + dot(waves[:, :width], low)
        return result * scale

    pairs = half // 2
    pair_copies = []
    for g in range(2):
        for p in range(pairs):
            if g == 0:
                loaded(other * half + 2 * p)
            sent[g, p] = coefficients(other * half + 2 * p, g)
            if g == 0 and p == 0:
                pl.semaphore_wait(barrier, len(friends))
            pair_copies.append(
                send(sent.at[g, p], got.at[g, p], pair_sem, len(pair_copies), device(core=other))
            )
    weight_copy = send(weight_hbm, weight.at[core], halo_sem, 1, device(core=other))

    edges = []

    def edge(source, target, where):
        edges.append(send(source, target, edge_sem, len(edges), where))

    edge(field_hbm.at[rows - 1], edged.at[0, pl.ds(PAD, width)], device(lat=south))
    edge(field_hbm.at[0], edged.at[rows + 1, pl.ds(PAD, width)], device(lat=north))
    edge(wet, wets.at[0, pl.ds(PAD, width)], device(lat=south))
    edge(wet, wets.at[2, pl.ds(PAD, width)], device(lat=north))

    low_lanes, high_lanes = pl.ds(0, cut), pl.ds(cut, cut)
    firsts = []
    for g in range(2):
        for p in range(pairs):
            if g == 0:
                loaded(core * half + 2 * p)
            mine = coefficients(core * half + 2 * p, g)
            pair_copies[g * pairs + p].wait_recv()
            mine = mine + got[g, p]
            sums[pl.ds(4 * g, 4), :, :, pl.ds(p * 256, 256)] = mine.reshape(4, xs, 8, 256)
        for n in range(4 * g, 4 * g + 4):
            firsts.append((
                send(sums.at[n, across, :, low_lanes], half_a.at[n], x_sem, n, device(x=right)),
                send(sums.at[n, across, :, high_lanes], half_b.at[n], x_sem, 8 + n, device(x=left)),
            ))
    middle = pl.ds(PAD, width)
    inner = [
        pltpu.make_async_copy(field, edged.at[pl.ds(1, rows), middle], local_sem.at[1]),
        pltpu.make_async_copy(wet, wets.at[1, middle], local_sem.at[2]),
    ]
    kept_table = pltpu.make_async_copy(turned, table_out, local_sem.at[11])
    for copy in inner + [kept_table]:
        copy.start()

    seconds = []
    for n in range(len(slices)):
        firsts[n][0].wait_recv()
        sums[n, right, :, low_lanes] = sums[n, right, :, low_lanes] + half_a[n]
        to_right = send(sums.at[n, right], full_a.at[n], x_sem, 16 + n, device(x=right))
        firsts[n][1].wait_recv()
        sums[n, left, :, high_lanes] = sums[n, left, :, high_lanes] + half_b[n]
        to_left = send(sums.at[n, left], full_b.at[n], x_sem, 24 + n, device(x=left))
        seconds.append((to_right, to_left))

    def send_edges():
        for copy in edges:
            copy.wait_recv()
        for copy in inner:
            copy.wait()
        for source, target, lon in ((PAD, PAD + width, west), (width, 0, east)):
            edge(edged.at[:, pl.ds(source, PAD)], edged.at[:, pl.ds(target, PAD)], device(**lon))
            edge(wets.at[:, pl.ds(source, PAD)], wets.at[:, pl.ds(target, PAD)], device(**lon))

    rising, falling = [], []
    for n in range(len(slices)):
        seconds[n][0].wait_recv()
        seconds[n][1].wait_recv()
        total = sums[n, x] + full_a[n] + full_b[n]
        if n == 0:
            part[n] = total
            rising.append(send(part.at[n, :, low_lanes], up.at[0, :, low_lanes], z_sem, 0, device(z=beyond)))
            falling.append(send(part.at[n, :, high_lanes], down.at[0, :, high_lanes], z_sem, 4, device(z=behind)))
            send_edges()
        elif n == 7:
            for buffer, chain in ((up, rising), (down, falling)):
                for hop in (2, 3):
                    chain[hop].wait_recv()
                    total = total + buffer[hop]
        else:
            rises = n % 2 == 1
            hop = (n + 1) // 2
            chain, buffer, span = (rising, up, low_lanes) if rises else (falling, down, high_lanes)
            near, far = (higher, beyond) if rises else (lower, behind)
            part[n] = total
            if hop == 2:
                chain[0].wait_recv()
                chain[1].wait_recv()
                part[n] = part[n] + buffer[1]
                part[n, :, span] = part[n, :, span] + buffer[0, :, span]
            chain.append(send(
                part.at[n], buffer.at[hop], z_sem, (0 if rises else 4) + hop,
                device(z=far if hop == 2 else near),
            ))

    own_weight.wait()
    weight_copy.wait_recv()
    terms = jnp.concatenate([total[:, i * 128 : (i + 1) * 128] for i in range(half)], 0)
    spot = lax.rem(lax.broadcasted_iota(jnp.int32, (half * 8, 128), 0), 8)
    real, imag = jnp.zeros((half * 8, 128), F32), jnp.zeros((half * 8, 128), F32)
    for m in range(4):
        chosen = (spot == 2 * m) | (spot == 2 * m + 1)
        picked = jnp.where(chosen, terms, 0.0)
        real = real + jnp.dot(picked, weight[m // 2, m % 2, 0], precision=HIGH, preferred_element_type=F32)
        imag = imag + jnp.dot(picked, weight[m // 2, m % 2, 1], precision=HIGH, preferred_element_type=F32)
    even = lax.rem(spot, 2) == 0
    mixed = real + jnp.where(even, -pltpu.roll(imag, half * 8 - 1, 0), pltpu.roll(imag, 1, 0))
    for i in range(half):
        whole[:, pl.ds(i * 128, 128)] = mixed[i * 8 : (i + 1) * 8]
    halo[...] = jnp.where(core == 0, mixed[:8], mixed[(half - 1) * 8 :])
    tail_lanes = pl.ds(lanes, 128)
    row_copy = send(halo, whole.at[:, tail_lanes], halo_sem, 0, device(lat=wrap(lat - 1 + 2 * core, lats)))
    kept = pltpu.make_async_copy(whole, mixed_out.at[core, z, x], local_sem.at[3])

    front, back = pl.ds(0, cut), pl.ds(cut, lanes + 128 - cut)
    order = (0, 7, 1, 6, 2, 5, 3, 4)
    slices = [wrap(z + step, zs) for step in order]
    sideways, relays, gathered = [], [], []

    def spread(n):
        zz = slices[n]
        mine = mixed_out.at[core, zz, x]
        source = whole if n == 0 else mine
        sideways.append((
            send(source, mine, gx_sem, n, device(x=right)),
            send(source, mine, gx_sem, 8 + n, device(x=left)),
        ))

    def relay(n):
        zz = slices[n]
        sideways[n][0].wait_recv()
        from_left = mixed_out.at[core, zz, left, :, front]
        first = send(from_left, from_left, gx_sem, 16 + n, device(x=right))
        sideways[n][1].wait_recv()
        from_right = mixed_out.at[core, zz, right, :, back]
        second = send(from_right, from_right, gx_sem, 24 + n, device(x=left))
        relays.append((first, second))

    def finish(n):
        zz = slices[n]
        relays[n][0].wait_recv()
        relays[n][1].wait_recv()
        if n == 0:
            kept.wait()
        done = mixed_out.at[core, zz]
        gathered.append(send(done, done, gp_sem, n, device(core=other)))

    def along(n, where, index, span=None):
        spot = mixed_out.at[core, slices[n], x]
        if span is not None:
            spot = mixed_out.at[core, slices[n], x, :, span]
        return send(whole.at[:, span] if n == 0 else spot, spot, gz_sem, index, device(z=where))

    paths = (beyond, behind, higher, lower)
    own = [along(0, where, index, pl.ds(0, lanes)) for index, where in enumerate(paths)]
    row_copy.wait_recv()
    kept.start()
    added = [along(0, where, 8 + index, tail_lanes) for index, where in enumerate(paths)]
    spread(0)
    own[2].wait_recv()
    added[2].wait_recv()
    spread(1)
    own[3].wait_recv()
    added[3].wait_recv()
    spread(2)
    own[0].wait_recv()
    added[0].wait_recv()
    next_up = along(3, higher, 4)
    half_up = along(3, beyond, 6, front)
    own[1].wait_recv()
    added[1].wait_recv()
    next_down = along(4, lower, 5)
    half_down = along(4, behind, 7, back)
    spread(3)
    spread(4)
    for n in range(3):
        relay(n)
    next_up.wait_recv()
    spread(5)
    next_down.wait_recv()
    spread(6)
    relay(3)
    relay(4)
    finish(0)
    half_up.wait_recv()
    half_down.wait_recv()
    spread(7)
    relay(5)
    finish(1)
    finish(2)
    relay(6)
    finish(3)
    finish(4)
    relay(7)
    for n in range(5, 8):
        finish(n)

    for copy in edges[4:] + gathered:
        copy.wait_recv()
    for copy in pending:
        copy.wait_send()
    kept_table.wait()


def exchange(field, ocean, modes, weight, lats, zs, xs, scale):
    rows, width, _ = field.shape
    wide = width + 2 * PAD
    lanes = rows // 2 * 128
    hbm = pl.BlockSpec(memory_space=pl.ANY)
    dma = pltpu.SemaphoreType.DMA
    return pl.pallas_call(
        functools.partial(exchange_kernel, zs, xs, lats, scale),
        out_shape=(
            jax.ShapeDtypeStruct((2, zs, xs, 8, lanes + 128), F32),
            jax.ShapeDtypeStruct((rows + 2, wide, 128), F32),
            jax.ShapeDtypeStruct((3, wide, 128), F32),
            jax.ShapeDtypeStruct((wide, 512), BF),
        ),
        in_specs=[hbm] * 4,
        out_specs=(hbm, hbm, hbm, hbm),
        scratch_shapes=[
            pltpu.VMEM(ocean.shape, jnp.int32),
            pltpu.VMEM((1, modes.size), jnp.int32),
            pltpu.VMEM((width, 128), F32),
            pltpu.VMEM((256, 2 * width), BF),
            pltpu.VMEM((wide, 512), BF),
            pltpu.VMEM((rows, width, 128), F32),
            pltpu.VMEM((2, *weight.shape), F32),
            pltpu.VMEM((2, rows // 4, 128, 256), F32),
            pltpu.VMEM((2, rows // 4, 128, 256), F32),
            pltpu.VMEM((zs, xs, 8, lanes), F32),
            pltpu.VMEM((zs, 8, lanes // 2), F32),
            pltpu.VMEM((zs, 8, lanes // 2), F32),
            pltpu.VMEM((zs, 8, lanes), F32),
            pltpu.VMEM((zs, 8, lanes), F32),
            pltpu.VMEM((zs, 8, lanes), F32),
            pltpu.VMEM((4, 8, lanes), F32),
            pltpu.VMEM((4, 8, lanes), F32),
            pltpu.VMEM((8, 128), F32),
            pltpu.VMEM((8, lanes + 128), F32),
            dma((rows,)), dma((2, 8)), dma((2, 32)), dma((2, 8)), dma((2, 2)), dma((2, 12)),
            dma((2, 32)), dma((2, 8)), dma((2, 8)), dma((14,)),
        ],
        compiler_params=pltpu.CompilerParams(
            collective_id=0, has_side_effects=True, vmem_limit_bytes=32 << 20
        ),
        name="exchange",
    )(*(pltpu.with_memory_space_constraint(a, pltpu.HBM) for a in (field, ocean, modes.reshape(1, -1), weight)))


def per_device(field, ocean, modes, spectral_weight, local_weight, layer_bias, conv_weight, conv_bias):
    rows, width, channels = field.shape
    lats, zs, xs = (lax.axis_size(name) for name in ("lat", "z", "x"))
    total_lon = width * zs * xs * 2
    total_modes = modes.shape[0]
    mixed, edged, wets, inverse = exchange(
        field, ocean, modes, spectral_weight, lats, zs, xs, 1.0 / math.sqrt(total_lon)
    )
    mixed = mixed.reshape(2, 2 * total_modes, -1)
    return tail(
        mixed, edged, wets, inverse, local_weight, layer_bias,
        conv_weight, conv_bias, rows, width, 2.0 / math.sqrt(total_modes), "lat", lats,
    )


def solution(mesh):
    split = Mesh(mesh.devices.reshape(mesh.shape["lat"], 8, 4, 2), ("lat", *LON))
    placed = (P("lat", LON, None), P("lat", LON), P(), P(LON, None, None, None), P(), P(), P(), P())
    return jax.shard_map(
        per_device, mesh=split, in_specs=placed, out_specs=P("lat", LON, None), check_vma=False
    )
```
